512 devices in a mesh: seq: 16 (over x, y), chan: 32 (over z, core).
Axes of the slice: x: 4, y: 4, z: 16, core: 2. Of those that a mesh axis runs over, the one named last changes fastest.
Arguments:
- stream: bfloat16 [16384, 8192], P('seq', 'chan'), may hold values from -80 to 80
- query_mr: bfloat16 [16384, 8192], P('seq', 'chan'), may hold values from -5 to 5
- key_mr: bfloat16 [16384, 8192], P('seq', 'chan'), may hold values from -5 to 5
- mr_filter: bfloat16 [128, 8192], P(None, 'chan'), may hold values from -0.5 to 0.5
- gain_mr: float32 [8192], P('chan'), may hold values from 0.5 to 1.5
- query_li: bfloat16 [16384, 8192], P('seq', 'chan'), may hold values from -5 to 5
- key_li: bfloat16 [16384, 8192], P('seq', 'chan'), may hold values from -5 to 5
- gain_li: float32 [8192], P('chan'), may hold values from 0.5 to 1.5
- decay_rate: float32 [16, 8192], P(None, 'chan'), may hold values from 0 to 1, as said below
- residue: float32 [16, 8192], P(None, 'chan'), may hold values from -3 to 3
- skip_weight: float32 [8192], P('chan'), may hold values from -1 to 1
Outputs:
- mr_output: bfloat16 [16384, 8192], P('seq', 'chan')
- li_output: bfloat16 [16384, 8192], P('seq', 'chan')
The draws below stay inside these ranges and needn't reach their ends.
Inputs may be any that keep to these rules, and one draw needn't show every extreme that they name: `decay_rate`: positive rates per position.
All inputs are finite; a program needn't handle non-finite values.
Results may differ from the reference program's by a relative error of at most 0.0085.
Values may be sent and summed in bfloat16 or wider, within the bound.
A program may use at most 64 MiB of HBM per device.

```python
import jax
import jax.numpy as jnp
from jax import lax

D = 8192
MODES = 16
MR_TAPS = 128
SEQ = 16384


def draw_stream(key, part):
    noise_key, row_key, col_key = jax.random.split(key, 3)
    positions = jnp.arange(D, dtype=jnp.float32) / D
    base_values = jnp.clip(jax.random.normal(noise_key, (SEQ, D), jnp.float32), -5.0, 5.0)
    row_scale = jnp.exp(jax.random.uniform(row_key, (SEQ, 1), jnp.float32) * jnp.log(10.0))
    col_scale = jnp.exp(jax.random.uniform(col_key, (1, D), jnp.float32) * jnp.log(10.0))
    ramp_scale = jnp.exp(0.5 * jnp.log(3.0) * positions)[None, :]
    return (base_values * row_scale * col_scale * ramp_scale / 20.0).astype(jnp.bfloat16)


def draw_decay_rate(key, part):
    fast_key = jax.random.fold_in(key, 1)
    lowest = jnp.log(0.1 / SEQ)
    highest = jnp.log(1.0 / 32.0)
    fast_rates = jnp.exp(jax.random.uniform(fast_key, (MODES, D), jnp.float32, lowest, highest))
    return fast_rates


def levels(own_key, shape, cuts, low, largest):
    loudness = 1.0
    for position, parts in cuts:
        draws = jax.random.uniform(jax.random.fold_in(jax.random.fold_in(own_key, 6), position), (parts,), jnp.float32, low / len(cuts), largest / len(cuts))
        loudness = loudness * jnp.repeat(jnp.exp(draws), shape[position] // parts).reshape((-1,) + (1,) * (len(shape) - 1 - position))
    return loudness


def bell_draw(key, extent, deviation, reach, pieces=(), kind=jnp.bfloat16):
    drawn = jax.random.normal(key, extent, jnp.float32) * deviation
    if len(pieces) > 0:
        drawn = levels(key, extent, pieces, -0.22, 0.18) * drawn
    return jnp.clip(drawn, min=-reach, max=reach).astype(kind)


def setup_inputs(seed: int = 0) -> dict:
    streams_of = jax.random.split(jax.random.key(seed), 12)
    return {
        "stream": draw_stream(jax.random.fold_in(streams_of[11], 71), 0),
        "query_mr": bell_draw(streams_of[1], (SEQ, D), 1.0, 5.0, ((0, 16), (1, 32))),
        "key_mr": bell_draw(streams_of[2], (SEQ, D), 1.0, 5.0, ((0, 16), (1, 32))),
        "mr_filter": bell_draw(streams_of[3], (MR_TAPS, D), MR_TAPS ** -0.5, 0.5, ((1, 32),)),
        "gain_mr": jnp.clip(1.0 + 0.1 * jax.random.normal(streams_of[4], (D,), jnp.float32), 0.5, 1.5),
        "query_li": bell_draw(streams_of[5], (SEQ, D), 1.0, 5.0, ((0, 16), (1, 32))),
        "key_li": bell_draw(streams_of[6], (SEQ, D), 1.0, 5.0, ((0, 16), (1, 32))),
        "gain_li": jnp.clip(1.0 + 0.1 * jax.random.normal(streams_of[7], (D,), jnp.float32), 0.5, 1.5),
        "decay_rate": draw_decay_rate(jax.random.fold_in(streams_of[11], 71), 0),
        "residue": bell_draw(streams_of[9], (MODES, D), 0.5, 3.0, ((1, 32),), jnp.float32),
        "skip_weight": jnp.clip(jax.random.uniform(streams_of[10], (D,), jnp.float32, -1.0, 1.0) * levels(streams_of[10], (D,), ((0, 32),), -0.4, 0.0), -1.0, 1.0),
    }


epsilon = 1e-06

def split_channels(array, blocks):
    return array.reshape(array.shape[0], blocks, array.shape[1] // blocks).transpose(1, 0, 2)

def join_channels(array):
    return array.transpose(1, 0, 2).reshape(array.shape[1], array.shape[0] * array.shape[2])

def causal_conv(signal, kernel_taps, length):
    fft_size = 2 * length
    spectrum = jnp.fft.rfft(signal, n=fft_size, axis=0) * jnp.fft.rfft(kernel_taps, n=fft_size, axis=0)
    return jnp.fft.irfft(spectrum, n=fft_size, axis=0)[:length]

def modal_filter(rates, weights, length):
    positions = jnp.arange(length, dtype=jnp.float32)
    scaled = weights * jnp.sqrt(-jnp.expm1(-2.0 * rates))
    return lax.optimization_barrier(jnp.sum(scaled[None] * jnp.exp(-rates[None] * positions[:, None, None]), axis=1))

def mr_block(items):
    signal, taps = items
    return causal_conv(signal, taps, SEQ)

def li_block(items):
    signal, rates, weights = items
    return causal_conv(signal, modal_filter(rates, weights, SEQ), SEQ)

def reference(stream, query_mr, key_mr, mr_filter, gain_mr, query_li, key_li, gain_li, decay_rate, residue, skip_weight):
    blocks = D // min(D, 128)
    wide_stream = stream.astype(jnp.float32)
    ms_mr = lax.optimization_barrier(jnp.mean(wide_stream * wide_stream, axis=1, keepdims=True))
    gated_mr = (key_mr.astype(jnp.float32) * (wide_stream * lax.rsqrt(ms_mr + epsilon) * gain_mr[None])).astype(jnp.bfloat16)
    conv_parts = lax.map(mr_block, (split_channels(gated_mr.astype(jnp.float32), blocks), split_channels(mr_filter.astype(jnp.float32), blocks)))
    conv_mr = join_channels(conv_parts)
    mr_output = (query_mr.astype(jnp.float32) * conv_mr).astype(jnp.bfloat16)
    mixed = (wide_stream + mr_output.astype(jnp.float32)).astype(jnp.bfloat16)
    mixed_wide = mixed.astype(jnp.float32)
    ms_li = lax.optimization_barrier(jnp.mean(mixed_wide * mixed_wide, axis=1, keepdims=True))
    value_li = key_li.astype(jnp.float32) * (mixed_wide * lax.rsqrt(ms_li + epsilon) * gain_li[None])
    long_parts = lax.map(li_block, (split_channels(value_li, blocks), split_channels(decay_rate, blocks), split_channels(residue, blocks)))
    conv_li = join_channels(long_parts)
    li_output = (query_li.astype(jnp.float32) * (conv_li + skip_weight[None] * value_li)).astype(jnp.bfloat16)
    return (mr_output, li_output)
```

```python
import functools

import jax
import jax.numpy as jnp
import numpy as np
from jax import lax
from jax.experimental import pallas as pl
from jax.experimental.pallas import tpu as pltpu
from jax.sharding import PartitionSpec as P

MESH = pl.DeviceIdType.MESH
F32 = jnp.float32
BF16 = jnp.bfloat16
epsilon = 1e-06

BLOCK = 128
POINTS = 2 * BLOCK
LANES = 128
HALF = 4


def transform_tables():
    turns = (2 * np.arange(BLOCK)[:, None] + 1) * np.arange(POINTS)[None, :] % (2 * POINTS)
    angle = turns * (np.pi / POINTS)
    forward = np.concatenate([np.cos(angle), -np.sin(angle)], axis=0)
    inverse = (2.0 / POINTS) * forward[:, BLOCK:].T

    def split(table):
        high = table.astype(BF16)
        low = (table - high.astype(np.float64)).astype(BF16)
        return np.concatenate([high, low, high], axis=1)

    return split(forward), split(forward[:, :BLOCK]), split(inverse)


def pieces(value):
    high = value.astype(BF16)
    low = (value - high.astype(F32)).astype(BF16)
    return jnp.concatenate([high, high, low], axis=0)


def matmul(a, b):
    return jnp.dot(a, b, preferred_element_type=F32)


def one_minus_exp(x):
    series = jnp.ones_like(x)
    for n in range(11, 1, -1):
        series = 1.0 - x * (1.0 / n) * series
    return jnp.where(x < 0.5, x * series, 1.0 - jnp.exp(-x))


def kernel(
    seq_count, chan_count, width,
    stream_h, qmr_h, kmr_h, taps_h, gmr_h, qli_h, kli_h, gli_h, lam_h, res_h, skip_h, fwd_h, fwda_h, inv_h,
    mr_h, li_h,
    stream, qmr, kmr, taps, gmr, qli, kli, gli, lam, res, skip, fwd, fwda, inv,
    mr, li, gated, mixed, value, rise, fall, segment, spec_h, spec_mr, spec_v, base,
    step_b, weight_b, norm, part, pair, own, gather, state, states,
    load_sem, store_sem, pair_send, pair_recv, far_send, far_recv, halo_send, halo_recv, state_send, state_recv,
):
    rows, chans = stream.shape
    blocks = rows // BLOCK
    modes = lam.shape[0]
    place = lax.axis_index("seq")
    chan = lax.axis_index("chan")
    core = lax.rem(chan, 2)
    partner = chan + 1 - 2 * core
    chips = chan_count // 2

    barrier = pltpu.get_barrier_semaphore()

    @pl.loop(1, chan_count)
    def _(i):
        pl.semaphore_signal(
            barrier, inc=1, device_id={"chan": lax.rem(chan + i, chan_count)}, device_id_type=MESH
        )

    @pl.loop(1, seq_count)
    def _(i):
        pl.semaphore_signal(
            barrier, inc=1, device_id={"seq": lax.rem(place + i, seq_count)}, device_id_type=MESH
        )

    loads = [
        pltpu.make_async_copy(source, target, load_sem.at[i])
        for i, (source, target) in enumerate(
            [
                (stream_h, stream), (lam_h, lam), (res_h, res), (taps_h, taps), (fwd_h, fwd), (fwda_h, fwda),
                (inv_h, inv), (kmr_h, kmr), (gmr_h, gmr), (qmr_h, qmr), (kli_h, kli), (gli_h, gli),
                (skip_h, skip), (qli_h, qli),
            ]
        )
    ]
    for load in loads:
        load.start()

    diagonal = (
        lax.broadcasted_iota(jnp.int32, (BLOCK, BLOCK), 0) == lax.broadcasted_iota(jnp.int32, (BLOCK, BLOCK), 1)
    )
    row_index = lax.broadcasted_iota(jnp.int32, (blocks, BLOCK), 0)

    def to_row(wide):
        total = jnp.sum(wide, axis=1, keepdims=True)
        return jnp.sum(jnp.where(diagonal, total, 0.0), axis=0, keepdims=True)

    def to_column(row):
        return jnp.sum(jnp.where(diagonal, row, 0.0), axis=1, keepdims=True)

    def block_rows(b):
        return pl.ds(pl.multiple_of(b * BLOCK, BLOCK), BLOCK)

    def reduce_start(which, sums):
        part[which, 0] = sums[:HALF]
        part[which, 1] = sums[HALF:]
        swap = pltpu.make_async_remote_copy(
            src_ref=part.at[which, 1 - core],
            dst_ref=pair.at[which],
            send_sem=pair_send.at[which],
            recv_sem=pair_recv.at[which],
            device_id={"chan": partner},
            device_id_type=MESH,
        )
        swap.start()
        swap.wait()
        mine = part[which, core] + pair[which]
        own[which] = mine
        gather[which, 0] = mine

        def send(chip_step, other):
            target = lax.rem(chan + 2 * chip_step, chan_count)
            target = target + other * (1 - 2 * core)
            slot = lax.rem(chips - chip_step, chips) * 2 + other
            pltpu.make_async_remote_copy(
                src_ref=own.at[which],
                dst_ref=gather.at[which, slot],
                send_sem=far_send.at[which],
                recv_sem=far_recv.at[which],
                device_id={"chan": target},
                device_id_type=MESH,
            ).start()

        order = sorted(range(1, chips), key=lambda d: -min(d, chips - d))
        for d in order:
            send(d, 0)
            send(d, 1)
        send(0, 1)

    def reduce_finish(which):
        others = gather.at[which, pl.ds(1, chan_count - 1)]
        pltpu.make_async_copy(others, others, far_recv.at[which]).wait()
        pltpu.make_async_copy(others, others, far_send.at[which]).wait()
        same = gather[which, 0]
        other = gather[which, 1]
        for d in range(1, chips):
            same = same + gather[which, 2 * d]
            other = other + gather[which, 2 * d + 1]
        norm[which, core] = lax.rsqrt(same * (1.0 / width) + epsilon)
        norm[which, 1 - core] = lax.rsqrt(other * (1.0 / width) + epsilon)

    loads[0].wait()

    def stream_sums(b, sums):
        wide = stream[block_rows(b), :].astype(F32)
        return jnp.where(row_index == b, to_row(wide * wide), sums)

    sums = lax.fori_loop(0, blocks, stream_sums, jnp.zeros((blocks, BLOCK), F32))

    loads[1].wait()
    loads[2].wait()
    rates = lam[...]
    weights = res[...] * jnp.sqrt(one_minus_exp(2.0 * rates))
    step_decay = jnp.exp(-float(BLOCK) * rates)
    offsets = lax.broadcasted_iota(jnp.int32, (BLOCK, chans), 0).astype(F32)
    for m in range(modes):
        step_b[m] = jnp.broadcast_to(step_decay[m : m + 1], (8, chans))
        weight_b[m] = jnp.broadcast_to(weights[m : m + 1], (8, chans))

    @pl.loop(0, modes)
    def _(m):
        rate = lam[pl.ds(m, 1), :]
        fall[m] = jnp.exp(-rate * offsets) * weight_b[m, 0:1]
        rise[m] = jnp.exp(-rate * (float(BLOCK - 1) - offsets))

    segment[0:BLOCK] = jnp.zeros((BLOCK, chans), F32)
    for tile in range(chans // LANES):
        lanes = slice(tile * LANES, (tile + 1) * LANES)

        @pl.loop(0, BLOCK // 8)
        def _(r):
            spot = pl.multiple_of(r * 8, 8)
            terms = [fall[m, pl.ds(spot, 8), lanes] for m in range(modes)]
            for b in range(blocks):
                total = terms[0]
                for m in range(1, modes):
                    total = total + terms[m]
                segment[pl.ds(pl.multiple_of((b + 1) * BLOCK + spot, 8), 8), lanes] = total
                if b < blocks - 1:
                    terms = [terms[m] * step_b[m, :, lanes] for m in range(modes)]

    pl.semaphore_wait(barrier, chan_count + seq_count - 2)
    reduce_start(0, sums)

    for load in loads[3:7]:
        load.wait()
    halves = taps[...]
    spec_mr[...] = matmul(fwda[:, : 2 * BLOCK], jnp.concatenate([halves, halves], axis=0))

    @pl.loop(0, blocks)
    def _(d):
        window = segment[pl.ds(pl.multiple_of(d * BLOCK, BLOCK), POINTS), :]
        spec_h[d] = matmul(fwd[...], pieces(window))

    for load in loads[7:10]:
        load.wait()
    reduce_finish(0)

    def gate(b):
        scale = to_column(norm[0, b // HALF, pl.ds(lax.rem(b, HALF), 1)])
        wide = stream[block_rows(b), :].astype(F32) * scale * gmr[...]
        gated[block_rows(b + 1), :] = (kmr[block_rows(b), :].astype(F32) * wide).astype(BF16)

    gate(jnp.int32(blocks - 1))
    halo = pltpu.make_async_remote_copy(
        src_ref=gated.at[pl.ds(rows, BLOCK)],
        dst_ref=gated.at[pl.ds(0, BLOCK)],
        send_sem=halo_send,
        recv_sem=halo_recv,
        device_id={"seq": lax.rem(place + 1, seq_count)},
        device_id_type=MESH,
    )

    @pl.when(place < seq_count - 1)
    def _():
        halo.start()

    @pl.when(place == 0)
    def _():
        gated[0:BLOCK] = jnp.zeros((BLOCK, chans), BF16)

    @pl.loop(0, blocks - 1)
    def _(b):
        gate(b)

    def mr_block(b, sums):
        window = gated[pl.ds(pl.multiple_of(b * BLOCK, BLOCK), POINTS), :]
        spec = matmul(fwd[:, : 2 * POINTS], jnp.concatenate([window, window], axis=0))
        re, im = spec[:BLOCK], spec[BLOCK:]
        tap_re, tap_im = spec_mr[:BLOCK], spec_mr[BLOCK:]
        product = jnp.concatenate([re * tap_re - im * tap_im, re * tap_im + im * tap_re], axis=0)
        conv = matmul(inv[...], pieces(product))
        here = block_rows(b)
        out = (qmr[here, :].astype(F32) * conv).astype(BF16)
        mr[here, :] = out
        mix = (stream[here, :].astype(F32) + out.astype(F32)).astype(BF16)
        mixed[here, :] = mix
        wide = mix.astype(F32)
        return jnp.where(row_index == b, to_row(wide * wide), sums)

    sums = lax.fori_loop(1, blocks, mr_block, jnp.zeros((blocks, BLOCK), F32))

    @pl.when(place > 0)
    def _():
        halo.wait_recv()

    sums = mr_block(jnp.int32(0), sums)
    reduce_start(1, sums)
    store_mr = pltpu.make_async_copy(mr, mr_h, store_sem.at[0])
    store_mr.start()
    for load in loads[10:]:
        load.wait()
    reduce_finish(1)

    @pl.loop(0, blocks)
    def _(b):
        scale = to_column(norm[1, b // HALF, pl.ds(lax.rem(b, HALF), 1)])
        here = block_rows(b)
        value[b] = kli[here, :].astype(F32) * (mixed[here, :].astype(F32) * scale * gli[...])

    for tile in range(chans // LANES):
        lanes = slice(tile * LANES, (tile + 1) * LANES)

        def collect(r, totals, lanes=lanes):
            spot = pl.ds(pl.multiple_of(r * 8, 8), 8)
            items = [value[b, spot, lanes] for b in range(blocks)]
            result = []
            for m in range(modes):
                decay = step_b[m, :, lanes]
                total = items[0]
                for b in range(1, blocks):
                    total = total * decay + items[b]
                result.append(totals[m] + total * rise[m, spot, lanes])
            return tuple(result)

        totals = lax.fori_loop(
            0, BLOCK // 8, collect, tuple(jnp.zeros((8, LANES), F32) for _ in range(modes))
        )
        for m in range(modes):
            state[m : m + 1, lanes] = jnp.sum(totals[m], axis=0, keepdims=True)

    def state_copy(target):
        return pltpu.make_async_remote_copy(
            src_ref=state,
            dst_ref=states.at[place],
            send_sem=state_send.at[target],
            recv_sem=state_recv.at[place],
            device_id={"seq": target},
            device_id_type=MESH,
        )

    @pl.loop(place + 1, seq_count)
    def _(target):
        state_copy(target).start()

    @pl.loop(0, blocks)
    def _(b):
        spec_v[b] = matmul(fwda[...], pieces(value[b]))

    for tile in range(chans // LANES):
        lanes = slice(tile * LANES, (tile + 1) * LANES)

        @pl.loop(0, BLOCK // 8)
        def _(r):
            upper = pl.ds(pl.multiple_of(r * 8, 8), 8)
            lower = pl.ds(pl.multiple_of(BLOCK + r * 8, 8), 8)
            h_re = [spec_h[d, upper, lanes] for d in range(blocks)]
            h_im = [spec_h[d, lower, lanes] for d in range(blocks)]
            v_re = [spec_v[b, upper, lanes] for b in range(blocks)]
            v_im = [spec_v[b, lower, lanes] for b in range(blocks)]
            for b in range(blocks):
                re = h_re[0] * v_re[b] - h_im[0] * v_im[b]
                im = h_re[0] * v_im[b] + h_im[0] * v_re[b]
                for d in range(1, b + 1):
                    re = re + (h_re[d] * v_re[b - d] - h_im[d] * v_im[b - d])
                    im = im + (h_re[d] * v_im[b - d] + h_im[d] * v_re[b - d])
                spec_v[b, upper, lanes] = re
                spec_v[b, lower, lanes] = im

    @pl.loop(0, blocks)
    def _(b):
        base[b] = matmul(inv[...], pieces(spec_v[b])) + skip[...] * value[b]

    through = jnp.exp(-float(rows) * rates)

    def take(q, total):
        pltpu.make_async_copy(states.at[q], states.at[q], state_recv.at[q]).wait()
        return total * through + states[q]

    incoming = lax.fori_loop(0, place, take, jnp.zeros((modes, chans), F32))
    lead = incoming * jnp.exp(-rates)
    for m in range(modes):
        weight_b[m] = jnp.broadcast_to(lead[m : m + 1], (8, chans))

    for tile in range(chans // LANES):
        lanes = slice(tile * LANES, (tile + 1) * LANES)

        @pl.loop(0, BLOCK // 16)
        def _(r):
            outs = [[None, None] for _ in range(blocks)]
            for part_index in range(2):
                spot = pl.ds(pl.multiple_of(r * 16 + part_index * 8, 8), 8)
                terms = [fall[m, spot, lanes] * weight_b[m, :, lanes] for m in range(modes)]
                for b in range(blocks):
                    total = base[b, spot, lanes]
                    for m in range(modes):
                        total = total + terms[m]
                    outs[b][part_index] = total
                    if b < blocks - 1:
                        terms = [terms[m] * step_b[m, :, lanes] for m in range(modes)]
            for b in range(blocks):
                here = pl.ds(pl.multiple_of(b * BLOCK + r * 16, 16), 16)
                total = jnp.concatenate(outs[b], axis=0)
                li[here, lanes] = (qli[here, lanes].astype(F32) * total).astype(BF16)

    store_li = pltpu.make_async_copy(li, li_h, store_sem.at[1])
    store_li.start()

    @pl.when(place < seq_count - 1)
    def _():
        halo.wait_send()

    @pl.loop(place + 1, seq_count)
    def _(target):
        state_copy(target).wait_send()

    store_mr.wait()
    store_li.wait()


def shards(seq_count, chan_count, width, *args):
    (stream, qmr, kmr, taps, gmr, qli, kli, gli, lam, res, skip) = args
    rows, chans = stream.shape
    modes = lam.shape[0]
    blocks = rows // BLOCK
    gmr, gli, skip = (a.reshape(1, chans) for a in (gmr, gli, skip))
    tables = transform_tables()
    operands = (stream, qmr, kmr, taps, gmr, qli, kli, gli, lam, res, skip) + tables
    vmem = pltpu.VMEM
    dma = pltpu.SemaphoreType.DMA
    return tuple(pl.pallas_call(
        functools.partial(kernel, seq_count, chan_count, width),
        out_shape=[jax.ShapeDtypeStruct((rows, chans), BF16)] * 2,
        in_specs=[pl.BlockSpec(memory_space=pl.ANY)] * len(operands),
        out_specs=[pl.BlockSpec(memory_space=pl.ANY)] * 2,
        scratch_shapes=[vmem(a.shape, a.dtype) for a in operands]
        + [
            vmem((rows, chans), BF16),
            vmem((rows, chans), BF16),
            vmem((rows + BLOCK, chans), BF16),
            vmem((rows, chans), BF16),
            vmem((blocks, BLOCK, chans), F32),
            vmem((modes, BLOCK, chans), F32),
            vmem((modes, BLOCK, chans), F32),
            vmem((rows + BLOCK, chans), F32),
            vmem((blocks, POINTS, chans), F32),
            vmem((POINTS, chans), F32),
            vmem((blocks, POINTS, chans), F32),
            vmem((blocks, BLOCK, chans), F32),
            vmem((modes, 8, chans), F32),
            vmem((modes, 8, chans), F32),
            vmem((2, 2, HALF, BLOCK), F32),
            vmem((2, 2, HALF, BLOCK), F32),
            vmem((2, HALF, BLOCK), F32),
            vmem((2, HALF, BLOCK), F32),
            vmem((2, chan_count, HALF, BLOCK), F32),
            vmem((modes, chans), F32),
            vmem((seq_count, modes, chans), F32),
            dma((len(operands),)),
            dma((2,)),
            dma((2,)),
            dma((2,)),
            dma((2,)),
            dma((2,)),
            dma,
            dma,
            dma((seq_count,)),
            dma((seq_count,)),
        ],
        compiler_params=pltpu.CompilerParams(collective_id=0, has_side_effects=True),
    )(*operands))


def solution(mesh):
    wide, per_channel, table = P("seq", "chan"), P("chan"), P(None, "chan")
    seq_count, chan_count = mesh.shape["seq"], mesh.shape["chan"]

    def whole(*args):
        width = args[0].shape[1]
        return jax.shard_map(
            functools.partial(shards, seq_count, chan_count, width),
            mesh=mesh,
            in_specs=(wide, wide, wide, table, per_channel, wide, wide, per_channel, table, table, per_channel),
            out_specs=(wide, wide),
            check_vma=False,
        )(*args)

    return whole
```

```python
import functools

import jax
import jax.numpy as jnp
import numpy as np
from jax import lax
from jax.experimental import pallas as pl
from jax.experimental.pallas import tpu as pltpu
from jax.sharding import PartitionSpec as P

MESH = pl.DeviceIdType.MESH
F32 = jnp.float32
BF16 = jnp.bfloat16
epsilon = 1e-06

BLOCK = 128
POINTS = 2 * BLOCK
LANES = 128


def transform_tables():
    turns = (2 * np.arange(BLOCK)[:, None] + 1) * np.arange(POINTS)[None, :] % (2 * POINTS)
    angle = turns * (np.pi / POINTS)
    forward = np.concatenate([np.cos(angle), -np.sin(angle)], axis=0)
    inverse = (2.0 / POINTS) * forward[:, BLOCK:].T
    high = forward.astype(BF16)
    low = (forward - high.astype(np.float64)).astype(BF16)
    return np.concatenate([high, low, high], axis=1), inverse.astype(BF16)


def pieces(value):
    high = value.astype(BF16)
    low = (value - high.astype(F32)).astype(BF16)
    return jnp.concatenate([high, high, low], axis=0)


def matmul(a, b):
    return jnp.dot(a, b, preferred_element_type=F32)


def one_minus_exp(x):
    series = jnp.ones_like(x)
    for n in range(11, 1, -1):
        series = 1.0 - x * (1.0 / n) * series
    return jnp.where(x < 0.5, x * series, 1.0 - jnp.exp(-x))


def main_kernel(
    seq_count, chan_count, width,
    stream_h, qmr_h, kmr_h, taps_h, gmr_h, qli_h, kli_h, gli_h, lam_h, res_h, skip_h, fwd_h, inv_h,
    mr, base, fall, lead_b, step_b, qli,
    stream, qmr, kmr, taps, gmr, kli, gli, lam, res, skip, fwd, inv,
    gated, mixed, value, rise, segment, spec_h, spec_mr, spec, product, weight_b,
    norm, own, gather, halo_stream, halo_kmr, edge, halo_edge, state, states,
    load_sem, far_send, far_recv, halo_send, halo_recv, state_send, state_recv,
):
    rows, chans = stream.shape
    blocks = rows // BLOCK
    modes = lam.shape[0]
    place = lax.axis_index("seq")
    chan = lax.axis_index("chan")
    core = lax.rem(chan, 2)
    chips = chan_count // 2

    loads = [
        pltpu.make_async_copy(source, target, load_sem.at[i])
        for i, (source, target) in enumerate(
            [
                (stream_h, stream), (lam_h, lam), (res_h, res), (taps_h, taps), (fwd_h, fwd), (inv_h, inv),
                (kmr_h, kmr), (gmr_h, gmr), (qmr_h, qmr), (kli_h, kli), (gli_h, gli), (skip_h, skip), (qli_h, qli),
            ]
        )
    ]
    loads[0].start()

    barrier = pltpu.get_barrier_semaphore()

    @pl.loop(1, chan_count)
    def _(i):
        pl.semaphore_signal(
            barrier, inc=1, device_id={"chan": lax.rem(chan + i, chan_count)}, device_id_type=MESH
        )

    @pl.loop(1, seq_count)
    def _(i):
        pl.semaphore_signal(
            barrier, inc=1, device_id={"seq": lax.rem(place + i, seq_count)}, device_id_type=MESH
        )

    for load in loads[1:]:
        load.start()

    diagonal = (
        lax.broadcasted_iota(jnp.int32, (BLOCK, BLOCK), 0) == lax.broadcasted_iota(jnp.int32, (BLOCK, BLOCK), 1)
    )

    def to_row(wide):
        total = jnp.sum(wide, axis=1, keepdims=True)
        return jnp.sum(jnp.where(diagonal, total, 0.0), axis=0, keepdims=True)

    def to_column(row):
        return jnp.sum(jnp.where(diagonal, row, 0.0), axis=1, keepdims=True)

    def block_rows(b):
        return slice(b * BLOCK, (b + 1) * BLOCK)

    def reduce_start(which):
        own[which] = norm[which].astype(BF16)

        def send(chip_step, other):
            target = lax.rem(chan + 2 * chip_step, chan_count) + other * (1 - 2 * core)
            slot = lax.rem(chips - chip_step, chips) * 2 + other - 1
            pltpu.make_async_remote_copy(
                src_ref=own.at[which],
                dst_ref=gather.at[which, slot],
                send_sem=far_send.at[which],
                recv_sem=far_recv.at[which],
                device_id={"chan": target},
                device_id_type=MESH,
            ).start()

        for d in sorted(range(1, chips), key=lambda d: -min(d, chips - d)):
            send(d, 0)
            send(d, 1)
        send(0, 1)

    def reduce_finish(which):
        others = gather.at[which]
        pltpu.make_async_copy(others, others, far_recv.at[which]).wait()
        terms = [norm[which]] + [gather[which, i].astype(F32) for i in range(chan_count - 1)]
        while len(terms) > 1:
            terms = [sum(terms[i : i + 2][1:], terms[i]) for i in range(0, len(terms), 2)]
        norm[which] = lax.rsqrt(terms[0] * (1.0 / width) + epsilon)

    loads[0].wait()
    for b in range(blocks):
        wide = stream[block_rows(b), :].astype(F32)
        norm[0, b : b + 1, :] = to_row(wide * wide)

    pl.semaphore_wait(barrier, chan_count + seq_count - 2)
    reduce_start(0)

    def to_next(source, target, i):
        return pltpu.make_async_remote_copy(
            src_ref=source,
            dst_ref=target,
            send_sem=halo_send.at[i],
            recv_sem=halo_recv.at[i],
            device_id={"seq": lax.rem(place + 1, seq_count)},
            device_id_type=MESH,
        )

    last = pl.ds(rows - BLOCK, BLOCK)
    halos = [
        to_next(stream_h.at[last], halo_stream, 0),
        to_next(kmr_h.at[last], halo_kmr, 1),
        to_next(edge, halo_edge, 2),
    ]

    @pl.when(place < seq_count - 1)
    def _():
        halos[0].start()
        halos[1].start()

    loads[1].wait()
    loads[2].wait()
    rates = lam[...]
    weights = res[...] * jnp.sqrt(one_minus_exp(2.0 * rates))
    step_decay = jnp.exp(-float(BLOCK) * rates)
    offsets = lax.broadcasted_iota(jnp.int32, (BLOCK, chans), 0).astype(F32)
    for m in range(modes):
        step_b[m] = jnp.broadcast_to(step_decay[m : m + 1], (8, chans))
        weight_b[m] = jnp.broadcast_to(weights[m : m + 1], (8, chans))

    @pl.loop(0, modes)
    def _(m):
        rate = lam[pl.ds(m, 1), :]
        fall[m] = jnp.exp(-rate * offsets) * weight_b[m, 0:1]
        rise[m] = jnp.exp(-rate * (float(BLOCK - 1) - offsets))

    segment[0:BLOCK] = jnp.zeros((BLOCK, chans), F32)
    for tile in range(chans // LANES):
        lanes = slice(tile * LANES, (tile + 1) * LANES)

        @pl.loop(0, BLOCK // 8)
        def _(r):
            spot = pl.multiple_of(r * 8, 8)
            terms = [fall[m, pl.ds(spot, 8), lanes] for m in range(modes)]
            for b in range(blocks):
                total = terms[0]
                for m in range(1, modes):
                    total = total + terms[m]
                segment[pl.ds(pl.multiple_of((b + 1) * BLOCK + spot, 8), 8), lanes] = total
                if b < blocks - 1:
                    terms = [terms[m] * step_b[m, :, lanes] for m in range(modes)]

    for load in loads[3:6]:
        load.wait()
    spec_mr[...] = matmul(fwd[:, :BLOCK], taps[...]) + matmul(fwd[:, POINTS : POINTS + BLOCK], taps[...])

    @pl.loop(0, blocks)
    def _(d):
        window = segment[pl.ds(pl.multiple_of(d * BLOCK, BLOCK), POINTS), :]
        spec_h[d] = matmul(fwd[...], pieces(window))

    for load in loads[6:9]:
        load.wait()
    reduce_finish(0)
    edge[...] = norm[0, blocks - 1 :, :]

    @pl.when(place < seq_count - 1)
    def _():
        halos[2].start()

    def gate(row, wide, key):
        wide = wide.astype(F32) * to_column(row) * gmr[...]
        return (key.astype(F32) * wide).astype(BF16)

    def gate_block(b):
        here = block_rows(b)
        gated[block_rows(b + 1), :] = gate(norm[0, b : b + 1, :], stream[here, :], kmr[here, :])

    def mr_block(b):
        spec[b] = matmul(fwd[:, :POINTS], gated[b * BLOCK : b * BLOCK + POINTS, :])
        for r in range(0, BLOCK, 16):
            upper, lower = slice(r, r + 16), slice(BLOCK + r, BLOCK + r + 16)
            re, im = spec[b, upper, :], spec[b, lower, :]
            tap_re, tap_im = spec_mr[upper, :], spec_mr[lower, :]
            product[b, upper, :] = (re * tap_re - im * tap_im).astype(BF16)
            product[b, lower, :] = (re * tap_im + im * tap_re).astype(BF16)
        conv = matmul(inv[...], product[b])
        here = block_rows(b)
        out = (qmr[here, :].astype(F32) * conv).astype(BF16)
        mr[here, :] = out
        mix = (stream[here, :].astype(F32) + out.astype(F32)).astype(BF16)
        mixed[here, :] = mix
        wide = mix.astype(F32)
        norm[1, b : b + 1, :] = to_row(wide * wide)

    gate_block(0)
    for b in range(1, blocks):
        gate_block(b)
        mr_block(b)

    @pl.when(place == 0)
    def _():
        gated[0:BLOCK] = jnp.zeros((BLOCK, chans), BF16)

    @pl.when(place > 0)
    def _():
        for halo in halos:
            halo.wait_recv()
        gated[0:BLOCK] = gate(halo_edge[...], halo_stream[...], halo_kmr[...])

    mr_block(0)
    reduce_start(1)
    for load in loads[9:]:
        load.wait()
    reduce_finish(1)

    for b in range(blocks):
        here = block_rows(b)
        scale = to_column(norm[1, b : b + 1, :])
        value[b] = kli[here, :].astype(F32) * (mixed[here, :].astype(F32) * scale * gli[...])

    for tile in range(chans // LANES):
        lanes = slice(tile * LANES, (tile + 1) * LANES)

        def collect(r, totals, lanes=lanes):
            spot = pl.ds(pl.multiple_of(r * 8, 8), 8)
            items = [value[b, spot, lanes] for b in range(blocks)]
            result = []
            for m in range(modes):
                decay = step_b[m, :, lanes]
                total = items[0]
                for b in range(1, blocks):
                    total = total * decay + items[b]
                result.append(totals[m] + total * rise[m, spot, lanes])
            return tuple(result)

        totals = lax.fori_loop(
            0, BLOCK // 8, collect, tuple(jnp.zeros((8, LANES), F32) for _ in range(modes))
        )
        for m in range(modes):
            state[m : m + 1, lanes] = jnp.sum(totals[m], axis=0, keepdims=True)

    def state_copy(target):
        return pltpu.make_async_remote_copy(
            src_ref=state,
            dst_ref=states.at[place],
            send_sem=state_send.at[target],
            recv_sem=state_recv.at[place],
            device_id={"seq": target},
            device_id_type=MESH,
        )

    @pl.loop(place + 1, seq_count)
    def _(target):
        state_copy(target).start()

    for b in range(blocks):
        spec[b] = matmul(fwd[:, :BLOCK], value[b].astype(BF16))

    for tile in range(chans // LANES):
        lanes = slice(tile * LANES, (tile + 1) * LANES)

        @pl.loop(0, BLOCK // 8)
        def _(r):
            upper = pl.ds(pl.multiple_of(r * 8, 8), 8)
            lower = pl.ds(pl.multiple_of(BLOCK + r * 8, 8), 8)
            h_re = [spec_h[d, upper, lanes] for d in range(blocks)]
            h_im = [spec_h[d, lower, lanes] for d in range(blocks)]
            v_re = [spec[b, upper, lanes] for b in range(blocks)]
            v_im = [spec[b, lower, lanes] for b in range(blocks)]
            for b in range(blocks):
                re = h_re[0] * v_re[b] - h_im[0] * v_im[b]
                im = h_re[0] * v_im[b] + h_im[0] * v_re[b]
                for d in range(1, b + 1):
                    re = re + (h_re[d] * v_re[b - d] - h_im[d] * v_im[b - d])
                    im = im + (h_re[d] * v_im[b - d] + h_im[d] * v_re[b - d])
                spec[b, upper, lanes] = re
                spec[b, lower, lanes] = im

    for b in range(blocks):
        base[b] = matmul(inv[...], spec[b].astype(BF16)) + skip[...] * value[b]

    through = jnp.exp(-float(rows) * rates)

    def take(q, total):
        pltpu.make_async_copy(states.at[q], states.at[q], state_recv.at[q]).wait()
        return total * through + states[q]

    incoming = lax.fori_loop(0, place, take, jnp.zeros((modes, chans), F32))
    lead = incoming * jnp.exp(-rates)
    for m in range(modes):
        lead_b[m] = jnp.broadcast_to(lead[m : m + 1], (8, chans))

    @pl.when(place < seq_count - 1)
    def _():
        for halo in halos:
            halo.wait_send()

    for which in range(2):
        others = gather.at[which]
        pltpu.make_async_copy(others, others, far_send.at[which]).wait()

    @pl.loop(place + 1, seq_count)
    def _(target):
        state_copy(target).wait_send()


def last_kernel(mr, base, fall, lead_b, step_b, qli, mr_h, li_h, li, store_sem):
    modes, _, chans = fall.shape
    blocks = base.shape[0]
    stores = [pltpu.make_async_copy(mr, mr_h, store_sem.at[0])]
    stores[0].start()
    for tile in range(chans // LANES):
        lanes = slice(tile * LANES, (tile + 1) * LANES)

        @pl.loop(0, BLOCK // 16)
        def _(r):
            outs = [[None, None] for _ in range(blocks)]
            for part_index in range(2):
                spot = pl.ds(pl.multiple_of(r * 16 + part_index * 8, 8), 8)
                terms = [fall[m, spot, lanes] * lead_b[m, :, lanes] for m in range(modes)]
                for b in range(blocks):
                    total = base[b, spot, lanes]
                    for m in range(modes):
                        total = total + terms[m]
                    outs[b][part_index] = total
                    if b < blocks - 1:
                        terms = [terms[m] * step_b[m, :, lanes] for m in range(modes)]
            for b in range(blocks):
                here = pl.ds(pl.multiple_of(b * BLOCK + r * 16, 16), 16)
                total = jnp.concatenate(outs[b], axis=0)
                li[here, lanes] = (qli[here, lanes].astype(F32) * total).astype(BF16)

        store = pltpu.make_async_copy(li.at[:, lanes], li_h.at[:, lanes], store_sem.at[1 + tile])
        store.start()
        stores.append(store)
    for store in stores:
        store.wait()


def shards(seq_count, chan_count, width, *args):
    (stream, qmr, kmr, taps, gmr, qli, kli, gli, lam, res, skip) = args
    rows, chans = stream.shape
    modes = lam.shape[0]
    blocks = rows // BLOCK
    gmr, gli, skip = (a.reshape(1, chans) for a in (gmr, gli, skip))
    operands = (stream, qmr, kmr, taps, gmr, qli, kli, gli, lam, res, skip) + transform_tables()
    vmem = pltpu.VMEM
    dma = pltpu.SemaphoreType.DMA
    passed = [
        vmem((rows, chans), BF16),
        vmem((blocks, BLOCK, chans), F32),
        vmem((modes, BLOCK, chans), F32),
        vmem((modes, 8, chans), F32),
        vmem((modes, 8, chans), F32),
        vmem((rows, chans), BF16),
    ]
    handed = pl.pallas_call(
        functools.partial(main_kernel, seq_count, chan_count, width),
        out_shape=passed,
        in_specs=[pl.BlockSpec(memory_space=pltpu.HBM)] * len(operands),
        out_specs=[pl.BlockSpec(memory_space=vmem)] * len(passed),
        scratch_shapes=[vmem(a.shape, a.dtype) for a in operands if a is not qli]
        + [
            vmem((rows + BLOCK, chans), BF16),
            vmem((rows, chans), BF16),
            vmem((blocks, BLOCK, chans), F32),
            vmem((modes, BLOCK, chans), F32),
            vmem((rows + BLOCK, chans), F32),
            vmem((blocks, POINTS, chans), F32),
            vmem((POINTS, chans), F32),
            vmem((blocks, POINTS, chans), F32),
            vmem((blocks, POINTS, chans), BF16),
            vmem((modes, 8, chans), F32),
            vmem((2, blocks, BLOCK), F32),
            vmem((2, blocks, BLOCK), BF16),
            vmem((2, chan_count - 1, blocks, BLOCK), BF16),
            vmem((BLOCK, chans), BF16),
            vmem((BLOCK, chans), BF16),
            vmem((1, BLOCK), F32),
            vmem((1, BLOCK), F32),
            vmem((modes, chans), F32),
            vmem((seq_count, modes, chans), F32),
            dma((len(operands),)),
            dma((2,)),
            dma((2,)),
            dma((3,)),
            dma((3,)),
            dma((seq_count,)),
            dma((seq_count,)),
        ],
        compiler_params=pltpu.CompilerParams(
            collective_id=0, has_side_effects=True, vmem_limit_bytes=36 * 2**20
        ),
    )(*(pltpu.with_memory_space_constraint(a, pltpu.HBM) for a in operands))
    return tuple(
        pl.pallas_call(
            last_kernel,
            out_shape=[jax.ShapeDtypeStruct((rows, chans), BF16)] * 2,
            in_specs=[pl.BlockSpec(memory_space=vmem)] * len(passed),
            out_specs=[pl.BlockSpec(memory_space=pltpu.HBM)] * 2,
            scratch_shapes=[vmem((rows, chans), BF16), dma((3,))],
            compiler_params=pltpu.CompilerParams(vmem_limit_bytes=8 * 2**20),
        )(*handed)
    )


def solution(mesh):
    wide, per_channel, table = P("seq", "chan"), P("chan"), P(None, "chan")
    seq_count, chan_count = mesh.shape["seq"], mesh.shape["chan"]

    def whole(*args):
        width = args[0].shape[1]
        return jax.shard_map(
            functools.partial(shards, seq_count, chan_count, width),
            mesh=mesh,
            in_specs=(wide, wide, wide, table, per_channel, wide, wide, per_channel, table, table, per_channel),
            out_specs=(wide, wide),
            check_vma=False,
        )(*args)

    return whole
```

```python
import functools

import jax
import jax.numpy as jnp
import numpy as np
from jax import lax
from jax.experimental import pallas as pl
from jax.experimental.pallas import tpu as pltpu
from jax.sharding import PartitionSpec as P

MESH = pl.DeviceIdType.MESH
F32 = jnp.float32
BF16 = jnp.bfloat16
epsilon = 1e-06

BLOCK = 128
POINTS = 2 * BLOCK
LANES = 128


def transform_tables():
    turns = (2 * np.arange(BLOCK)[:, None] + 1) * np.arange(POINTS)[None, :] % (2 * POINTS)
    angle = turns * (np.pi / POINTS)
    forward = np.concatenate([np.cos(angle), -np.sin(angle)], axis=0)
    inverse = (2.0 / POINTS) * forward[:, BLOCK:].T
    high = forward.astype(BF16)
    low = (forward - high.astype(np.float64)).astype(BF16)
    return np.concatenate([high, low, high], axis=1), inverse.astype(BF16)


def pieces(value):
    high = value.astype(BF16)
    low = (value - high.astype(F32)).astype(BF16)
    return jnp.concatenate([high, high, low], axis=0)


def matmul(a, b):
    return jnp.dot(a, b, preferred_element_type=F32)


def one_minus_exp(x):
    series = jnp.ones_like(x)
    for n in range(11, 1, -1):
        series = 1.0 - x * (1.0 / n) * series
    return jnp.where(x < 0.5, x * series, 1.0 - jnp.exp(-x))


def main_kernel(
    seq_count, chan_count, width,
    stream_h, qmr_h, kmr_h, taps_h, gmr_h, qli_h, kli_h, gli_h, lam_h, res_h, skip_h, fwd_h, inv_h,
    mr, base, fall, lead_b, step_b, qli,
    stream, qmr, kmr, taps, gmr, kli, gli, lam, res, skip, fwd, inv,
    gated, mixed, value, rise, segment, spec_h, spec_mr, spec, product, weight_b, leap_b, raw_halo, scale, held,
    norm, own, gather, own_first, gather_first, halo_stream, halo_kmr, edge, halo_edge, state_wide, state, states,
    load_sem, far_send, far_recv, halo_send, halo_recv, state_send, state_recv,
):
    rows, chans = stream.shape
    blocks = rows // BLOCK
    modes = lam.shape[0]
    place = lax.axis_index("seq")
    chan = lax.axis_index("chan")
    core = lax.rem(chan, 2)
    chips = chan_count // 2

    loads = [
        pltpu.make_async_copy(source, target, load_sem.at[i])
        for i, (source, target) in enumerate(
            [
                (stream_h, stream), (lam_h, lam), (res_h, res), (taps_h, taps), (fwd_h, fwd), (inv_h, inv),
                (kmr_h, kmr), (gmr_h, gmr), (qmr_h, qmr), (kli_h, kli), (gli_h, gli), (skip_h, skip), (qli_h, qli),
            ]
        )
    ]
    loads[0].start()

    barrier = pltpu.get_barrier_semaphore()

    farthest_first = sorted(range(1, chips), key=lambda d: -min(d, chips - d))

    def peer(chip_step, other):
        return {"chan": lax.rem(chan + 2 * chip_step, chan_count) + other * (1 - 2 * core)}

    for d, other in [(d, other) for d in farthest_first for other in (0, 1)] + [(0, 1)]:
        pl.semaphore_signal(barrier, inc=1, device_id=peer(d, other), device_id_type=MESH)

    @pl.loop(1, seq_count)
    def _(i):
        pl.semaphore_signal(
            barrier, inc=1, device_id={"seq": lax.rem(place + i, seq_count)}, device_id_type=MESH
        )

    for load in loads[1:]:
        load.start()

    diagonal = (
        lax.broadcasted_iota(jnp.int32, (BLOCK, BLOCK), 0) == lax.broadcasted_iota(jnp.int32, (BLOCK, BLOCK), 1)
    )

    def to_row(wide):
        total = jnp.sum(wide, axis=1, keepdims=True)
        return jnp.sum(jnp.where(diagonal, total, 0.0), axis=0, keepdims=True)

    def to_column(row):
        return jnp.sum(jnp.where(diagonal, row, 0.0), axis=1, keepdims=True)

    def block_rows(b):
        return slice(b * BLOCK, (b + 1) * BLOCK)

    def reduce_start(which, source, target):
        for d, other in [(d, other) for d in farthest_first for other in (0, 1)] + [(0, 1)]:
            slot = (chips - d) % chips * 2 + other - 1
            pltpu.make_async_remote_copy(
                src_ref=source,
                dst_ref=target.at[slot],
                send_sem=far_send.at[which],
                recv_sem=far_recv.at[which],
                device_id=peer(d, other),
                device_id_type=MESH,
            ).start()

    def reduce_finish(which, mine, target):
        pltpu.make_async_copy(target, target, far_recv.at[which]).wait()
        terms = [mine] + [target[i].astype(F32) for i in range(chan_count - 1)]
        while len(terms) > 1:
            terms = [sum(terms[i + 1 : i + 2], terms[i]) for i in range(0, len(terms), 2)]
        return lax.rsqrt(terms[0] * (1.0 / width) + epsilon)

    loads[0].wait()
    for b in range(blocks):
        wide = stream[block_rows(b), :].astype(F32)
        norm[0, b : b + 1, :] = to_row(wide * wide)

    pl.semaphore_wait(barrier, chan_count + seq_count - 2)
    own[0] = norm[0].astype(BF16)
    reduce_start(0, own.at[0], gather.at[0])

    def to_next(source, target, i):
        return pltpu.make_async_remote_copy(
            src_ref=source,
            dst_ref=target,
            send_sem=halo_send.at[i],
            recv_sem=halo_recv.at[i],
            device_id={"seq": lax.rem(place + 1, seq_count)},
            device_id_type=MESH,
        )

    last = pl.ds(rows - BLOCK, BLOCK)
    halos = [
        to_next(stream_h.at[last], halo_stream, 0),
        to_next(kmr_h.at[last], halo_kmr, 1),
        to_next(edge, halo_edge, 2),
    ]

    @pl.when(place < seq_count - 1)
    def _():
        halos[0].start()
        halos[1].start()

    loads[1].wait()
    loads[2].wait()
    rates = lam[...]
    weights = res[...] * jnp.sqrt(one_minus_exp(2.0 * rates))
    step_decay = jnp.exp(-float(BLOCK) * rates)
    leap = jnp.exp(-float(rows - BLOCK) * rates)
    offsets = lax.broadcasted_iota(jnp.int32, (BLOCK, chans), 0).astype(F32)
    for m in range(modes):
        step_b[m] = jnp.broadcast_to(step_decay[m : m + 1], (8, chans))
        weight_b[m] = jnp.broadcast_to(weights[m : m + 1], (8, chans))
        leap_b[m] = jnp.broadcast_to(leap[m : m + 1], (8, chans))

    @pl.loop(0, modes)
    def _(m):
        rate = lam[pl.ds(m, 1), :]
        fall[m] = jnp.exp(-rate * offsets) * weight_b[m, 0:1]
        rise[m] = jnp.exp(-rate * (float(BLOCK - 1) - offsets))

    segment[0:BLOCK] = jnp.zeros((BLOCK, chans), F32)
    for tile in range(chans // LANES):
        lanes = slice(tile * LANES, (tile + 1) * LANES)

        @pl.loop(0, BLOCK // 8)
        def _(r):
            spot = pl.multiple_of(r * 8, 8)
            terms = [fall[m, pl.ds(spot, 8), lanes] for m in range(modes)]
            for b in range(blocks):
                total = terms[0]
                for m in range(1, modes):
                    total = total + terms[m]
                segment[pl.ds(pl.multiple_of((b + 1) * BLOCK + spot, 8), 8), lanes] = total
                if b < blocks - 1:
                    terms = [terms[m] * step_b[m, :, lanes] for m in range(modes)]

    for load in loads[3:6]:
        load.wait()
    spec_mr[...] = matmul(fwd[:, :BLOCK], taps[...]) + matmul(fwd[:, POINTS : POINTS + BLOCK], taps[...])

    @pl.loop(0, blocks)
    def _(d):
        window = segment[pl.ds(pl.multiple_of(d * BLOCK, BLOCK), POINTS), :]
        spec_h[d] = matmul(fwd[...], pieces(window))

    for load in loads[6:9]:
        load.wait()
    for b in range(blocks):
        here = block_rows(b)
        value[b] = kmr[here, :].astype(F32) * (stream[here, :].astype(F32) * gmr[...])

    @pl.when(place > 0)
    def _():
        halos[0].wait_recv()
        halos[1].wait_recv()
        raw_halo[...] = halo_kmr[...].astype(F32) * (halo_stream[...].astype(F32) * gmr[...])

    norm[0] = reduce_finish(0, norm[0], gather.at[0])
    edge[...] = norm[0, blocks - 1 :, :]

    @pl.when(place < seq_count - 1)
    def _():
        halos[2].start()

    def gate_block(b):
        gated[block_rows(b + 1), :] = (value[b] * to_column(norm[0, b : b + 1, :])).astype(BF16)

    def mr_block(b):
        spec[b] = matmul(fwd[:, :POINTS], gated[b * BLOCK : b * BLOCK + POINTS, :])
        for r in range(0, BLOCK, 16):
            upper, lower = slice(r, r + 16), slice(BLOCK + r, BLOCK + r + 16)
            re, im = spec[b, upper, :], spec[b, lower, :]
            tap_re, tap_im = spec_mr[upper, :], spec_mr[lower, :]
            product[b, upper, :] = (re * tap_re - im * tap_im).astype(BF16)
            product[b, lower, :] = (re * tap_im + im * tap_re).astype(BF16)
        conv = matmul(inv[...], product[b])
        here = block_rows(b)
        out = (qmr[here, :].astype(F32) * conv).astype(BF16)
        mr[here, :] = out
        mix = (stream[here, :].astype(F32) + out.astype(F32)).astype(BF16)
        mixed[here, :] = mix
        wide = mix.astype(F32)
        norm[1, b : b + 1, :] = to_row(wide * wide)

    gate_block(0)
    for b in range(1, blocks):
        gate_block(b)
        mr_block(b)
    norm[1, 0:1, :] = jnp.zeros((1, BLOCK), F32)
    own[1] = norm[1].astype(BF16)
    reduce_start(1, own.at[1], gather.at[1])

    @pl.when(place == 0)
    def _():
        gated[0:BLOCK] = jnp.zeros((BLOCK, chans), BF16)

    @pl.when(place > 0)
    def _():
        halos[2].wait_recv()
        gated[0:BLOCK] = (raw_halo[...] * to_column(halo_edge[...])).astype(BF16)

    mr_block(0)
    own_first[...] = norm[1, 0:1, :]
    reduce_start(2, own_first, gather_first)

    for load in loads[9:]:
        load.wait()
    for b in range(blocks):
        here = block_rows(b)
        value[b] = kli[here, :].astype(F32) * (mixed[here, :].astype(F32) * gli[...])

    def widen(row):
        return jnp.broadcast_to(to_column(row), (BLOCK, LANES))

    norm[1] = reduce_finish(1, norm[1], gather.at[1])
    for b in range(1, blocks):
        scale[b] = widen(norm[1, b : b + 1, :])

    for tile in range(chans // LANES):
        lanes = slice(tile * LANES, (tile + 1) * LANES)

        def collect(r, totals, lanes=lanes):
            spot = pl.ds(pl.multiple_of(r * 8, 8), 8)
            items = [value[b, spot, lanes] * scale[b, spot, :] for b in range(1, blocks)]
            result = []
            for m in range(modes):
                decay = step_b[m, :, lanes]
                total = items[0]
                for item in items[1:]:
                    total = total * decay + item
                result.append(totals[m] + total * rise[m, spot, lanes])
            return tuple(result)

        totals = lax.fori_loop(
            0, BLOCK // 8, collect, tuple(jnp.zeros((8, LANES), F32) for _ in range(modes))
        )
        for m in range(modes):
            held[m, :, lanes] = totals[m]

    scale[0] = widen(reduce_finish(2, own_first[...], gather_first))

    def state_copy(target):
        return pltpu.make_async_remote_copy(
            src_ref=state,
            dst_ref=states.at[place],
            send_sem=state_send.at[target],
            recv_sem=state_recv.at[place],
            device_id={"seq": target},
            device_id_type=MESH,
        )

    for tile in range(chans // LANES):
        lanes = slice(tile * LANES, (tile + 1) * LANES)

        def collect_first(r, totals, lanes=lanes):
            spot = pl.ds(pl.multiple_of(r * 8, 8), 8)
            item = value[0, spot, lanes] * scale[0, spot, :]
            return tuple(totals[m] + item * rise[m, spot, lanes] for m in range(modes))

        totals = lax.fori_loop(
            0, BLOCK // 8, collect_first, tuple(jnp.zeros((8, LANES), F32) for _ in range(modes)), unroll=2
        )
        for m in range(modes):
            total = held[m, :, lanes] + totals[m] * leap_b[m, :, lanes]
            state_wide[m : m + 1, :] = jnp.sum(total, axis=0, keepdims=True)
        state[tile] = state_wide[...].astype(BF16)

    @pl.loop(place + 1, seq_count)
    def _(target):
        state_copy(target).start()

    for b in range(blocks):
        value[b] = value[b] * jnp.concatenate([scale[b]] * (chans // LANES), axis=1)
        spec[b] = matmul(fwd[:, :BLOCK], value[b].astype(BF16))

    for tile in range(chans // LANES):
        lanes = slice(tile * LANES, (tile + 1) * LANES)

        @pl.loop(0, BLOCK // 8)
        def _(r):
            upper = pl.ds(pl.multiple_of(r * 8, 8), 8)
            lower = pl.ds(pl.multiple_of(BLOCK + r * 8, 8), 8)
            h_re = [spec_h[d, upper, lanes] for d in range(blocks)]
            h_im = [spec_h[d, lower, lanes] for d in range(blocks)]
            v_re = [spec[b, upper, lanes] for b in range(blocks)]
            v_im = [spec[b, lower, lanes] for b in range(blocks)]
            for b in range(blocks):
                re = h_re[0] * v_re[b] - h_im[0] * v_im[b]
                im = h_re[0] * v_im[b] + h_im[0] * v_re[b]
                for d in range(1, b + 1):
                    re = re + (h_re[d] * v_re[b - d] - h_im[d] * v_im[b - d])
                    im = im + (h_re[d] * v_im[b - d] + h_im[d] * v_re[b - d])
                spec[b, upper, lanes] = re
                spec[b, lower, lanes] = im

    for b in range(blocks):
        base[b] = matmul(inv[...], spec[b].astype(BF16)) + skip[...] * value[b]

    through = jnp.exp(-float(rows) * rates)

    def take(q, totals):
        pltpu.make_async_copy(states.at[q], states.at[q], state_recv.at[q]).wait()
        return tuple(
            total * through[:, tile * LANES : (tile + 1) * LANES] + states[q, tile].astype(F32)
            for tile, total in enumerate(totals)
        )

    tiles = range(chans // LANES)
    incoming = lax.fori_loop(0, place, take, tuple(jnp.zeros((modes, LANES), F32) for _ in tiles))
    for tile in tiles:
        lanes = slice(tile * LANES, (tile + 1) * LANES)
        lead = incoming[tile] * jnp.exp(-rates[:, lanes])
        for m in range(modes):
            lead_b[m, :, lanes] = jnp.broadcast_to(lead[m : m + 1], (8, LANES))

    @pl.when(place < seq_count - 1)
    def _():
        for halo in halos:
            halo.wait_send()

    for which, others in enumerate((gather.at[0], gather.at[1], gather_first)):
        pltpu.make_async_copy(others, others, far_send.at[which]).wait()

    @pl.loop(place + 1, seq_count)
    def _(target):
        state_copy(target).wait_send()


def last_kernel(mr, base, fall, lead_b, step_b, qli, mr_h, li_h, li, store_sem):
    modes, _, chans = fall.shape
    blocks = base.shape[0]
    stores = [pltpu.make_async_copy(mr, mr_h, store_sem.at[0])]
    stores[0].start()
    for tile in range(chans // LANES):
        lanes = slice(tile * LANES, (tile + 1) * LANES)

        @pl.loop(0, BLOCK // 16)
        def _(r):
            outs = [[None, None] for _ in range(blocks)]
            for part_index in range(2):
                spot = pl.ds(pl.multiple_of(r * 16 + part_index * 8, 8), 8)
                totals = [base[b, spot, lanes] for b in range(blocks)]
                for group in (range(modes // 2), range(modes // 2, modes)):
                    terms = [fall[m, spot, lanes] * lead_b[m, :, lanes] for m in group]
                    steps = [step_b[m, :, lanes] for m in group]
                    for b in range(blocks):
                        pairs = terms
                        while len(pairs) > 1:
                            pairs = [sum(pairs[i + 1 : i + 2], pairs[i]) for i in range(0, len(pairs), 2)]
                        totals[b] = totals[b] + pairs[0]
                        if b < blocks - 1:
                            terms = [term * step for term, step in zip(terms, steps)]
                for b in range(blocks):
                    outs[b][part_index] = totals[b]
            for b in range(blocks):
                here = pl.ds(pl.multiple_of(b * BLOCK + r * 16, 16), 16)
                total = jnp.concatenate(outs[b], axis=0)
                li[here, lanes] = (qli[here, lanes].astype(F32) * total).astype(BF16)

        store = pltpu.make_async_copy(li.at[:, lanes], li_h.at[:, lanes], store_sem.at[1 + tile])
        store.start()
        stores.append(store)
    for store in stores:
        store.wait()


def shards(seq_count, chan_count, width, *args):
    (stream, qmr, kmr, taps, gmr, qli, kli, gli, lam, res, skip) = args
    rows, chans = stream.shape
    modes = lam.shape[0]
    blocks = rows // BLOCK
    gmr, gli, skip = (a.reshape(1, chans) for a in (gmr, gli, skip))
    operands = (stream, qmr, kmr, taps, gmr, qli, kli, gli, lam, res, skip) + transform_tables()
    vmem = pltpu.VMEM
    dma = pltpu.SemaphoreType.DMA
    passed = [
        vmem((rows, chans), BF16),
        vmem((blocks, BLOCK, chans), F32),
        vmem((modes, BLOCK, chans), F32),
        vmem((modes, 8, chans), F32),
        vmem((modes, 8, chans), F32),
        vmem((rows, chans), BF16),
    ]
    handed = pl.pallas_call(
        functools.partial(main_kernel, seq_count, chan_count, width),
        out_shape=passed,
        in_specs=[pl.BlockSpec(memory_space=pltpu.HBM)] * len(operands),
        out_specs=[pl.BlockSpec(memory_space=vmem)] * len(passed),
        scratch_shapes=[vmem(a.shape, a.dtype) for a in operands if a is not qli]
        + [
            vmem((rows + BLOCK, chans), BF16),
            vmem((rows, chans), BF16),
            vmem((blocks, BLOCK, chans), F32),
            vmem((modes, BLOCK, chans), F32),
            vmem((rows + BLOCK, chans), F32),
            vmem((blocks, POINTS, chans), F32),
            vmem((POINTS, chans), F32),
            vmem((blocks, POINTS, chans), F32),
            vmem((blocks, POINTS, chans), BF16),
            vmem((modes, 8, chans), F32),
            vmem((modes, 8, chans), F32),
            vmem((BLOCK, chans), F32),
            vmem((blocks, BLOCK, LANES), F32),
            vmem((modes, 8, chans), F32),
            vmem((2, blocks, BLOCK), F32),
            vmem((2, blocks, BLOCK), BF16),
            vmem((2, chan_count - 1, blocks, BLOCK), BF16),
            vmem((1, BLOCK), F32),
            vmem((chan_count - 1, 1, BLOCK), F32),
            vmem((BLOCK, chans), BF16),
            vmem((BLOCK, chans), BF16),
            vmem((1, BLOCK), F32),
            vmem((1, BLOCK), F32),
            vmem((modes, LANES), F32),
            vmem((chans // LANES, modes, LANES), BF16),
            vmem((seq_count, chans // LANES, modes, LANES), BF16),
            dma((len(operands),)),
            dma((3,)),
            dma((3,)),
            dma((3,)),
            dma((3,)),
            dma((seq_count,)),
            dma((seq_count,)),
        ],
        compiler_params=pltpu.CompilerParams(
            collective_id=0, has_side_effects=True, vmem_limit_bytes=36 * 2**20
        ),
    )(*(pltpu.with_memory_space_constraint(a, pltpu.HBM) for a in operands))
    return tuple(
        pl.pallas_call(
            last_kernel,
            out_shape=[jax.ShapeDtypeStruct((rows, chans), BF16)] * 2,
            in_specs=[pl.BlockSpec(memory_space=vmem)] * len(passed),
            out_specs=[pl.BlockSpec(memory_space=pltpu.HBM)] * 2,
            scratch_shapes=[vmem((rows, chans), BF16), dma((3,))],
            compiler_params=pltpu.CompilerParams(vmem_limit_bytes=8 * 2**20),
        )(*handed)
    )


def solution(mesh):
    wide, per_channel, table = P("seq", "chan"), P("chan"), P(None, "chan")
    seq_count, chan_count = mesh.shape["seq"], mesh.shape["chan"]

    def whole(*args):
        width = args[0].shape[1]
        return jax.shard_map(
            functools.partial(shards, seq_count, chan_count, width),
            mesh=mesh,
            in_specs=(wide, wide, wide, table, per_channel, wide, wide, per_channel, table, table, per_channel),
            out_specs=(wide, wide),
            check_vma=False,
        )(*args)

    return whole
```

```python
import functools

import jax
import jax.numpy as jnp
import numpy as np
from jax import lax
from jax.experimental import pallas as pl
from jax.experimental.pallas import tpu as pltpu
from jax.sharding import PartitionSpec as P

MESH = pl.DeviceIdType.MESH
F32 = jnp.float32
BF16 = jnp.bfloat16
epsilon = 1e-06

BLOCK = 128
POINTS = 2 * BLOCK
LANES = 128


def transform_tables():
    turns = (2 * np.arange(BLOCK)[:, None] + 1) * np.arange(POINTS)[None, :] % (2 * POINTS)
    angle = turns * (np.pi / POINTS)
    forward = np.concatenate([np.cos(angle), -np.sin(angle)], axis=0)
    inverse = (2.0 / POINTS) * forward[:, BLOCK:].T
    high = forward.astype(BF16)
    low = (forward - high.astype(np.float64)).astype(BF16)
    return np.concatenate([high, low, high], axis=1), inverse.astype(BF16)


def pieces(value):
    high = value.astype(BF16)
    low = (value - high.astype(F32)).astype(BF16)
    return jnp.concatenate([high, high, low], axis=0)


def matmul(a, b):
    return jnp.dot(a, b, preferred_element_type=F32)


def one_minus_exp(x):
    series = jnp.ones_like(x)
    for n in range(11, 1, -1):
        series = 1.0 - x * (1.0 / n) * series
    return jnp.where(x < 0.5, x * series, 1.0 - jnp.exp(-x))


def main_kernel(
    seq_count, chan_count, width,
    stream_h, qmr_h, kmr_h, taps_h, gmr_h, qli_h, kli_h, gli_h, lam_h, res_h, skip_h, fwd_h, inv_h,
    mr, base, fall, lead_b, step_b, qli,
    stream, qmr, kmr, taps, gmr, kli, gli, lam, res, skip, fwd, inv,
    gated, mixed, value, rise, segment, spec_h, spec_mr, spec, product, weight_b, leap_b, raw_halo, scale, held,
    norm, own, gather, own_first, gather_first, halo_stream, halo_kmr, edge, halo_edge, state_wide, state, states,
    load_sem, far_send, far_recv, halo_send, halo_recv, state_send, state_recv,
):
    rows, chans = stream.shape
    blocks = rows // BLOCK
    modes = lam.shape[0]
    place = lax.axis_index("seq")
    chan = lax.axis_index("chan")
    core = lax.rem(chan, 2)
    chips = chan_count // 2

    loads = [
        pltpu.make_async_copy(source, target, load_sem.at[i])
        for i, (source, target) in enumerate(
            [
                (stream_h, stream), (lam_h, lam), (res_h, res), (taps_h, taps), (fwd_h, fwd), (inv_h, inv),
                (kmr_h, kmr), (gmr_h, gmr), (qmr_h, qmr), (kli_h, kli), (gli_h, gli), (skip_h, skip), (qli_h, qli),
            ]
        )
    ]
    loads[0].start()

    barrier = pltpu.get_barrier_semaphore()

    farthest_first = sorted(range(1, chips), key=lambda d: -min(d, chips - d))

    def peer(chip_step, other):
        return {"chan": lax.rem(chan + 2 * chip_step, chan_count) + other * (1 - 2 * core)}

    for d, other in [(d, other) for d in farthest_first for other in (0, 1)] + [(0, 1)]:
        pl.semaphore_signal(barrier, inc=1, device_id=peer(d, other), device_id_type=MESH)

    @pl.loop(1, seq_count)
    def _(i):
        pl.semaphore_signal(
            barrier, inc=1, device_id={"seq": lax.rem(place + i, seq_count)}, device_id_type=MESH
        )

    for load in loads[1:]:
        load.start()

    diagonal = (
        lax.broadcasted_iota(jnp.int32, (BLOCK, BLOCK), 0) == lax.broadcasted_iota(jnp.int32, (BLOCK, BLOCK), 1)
    )

    def to_row(wide):
        total = jnp.sum(wide, axis=1, keepdims=True)
        return jnp.sum(jnp.where(diagonal, total, 0.0), axis=0, keepdims=True)

    def to_column(row):
        return jnp.sum(jnp.where(diagonal, row, 0.0), axis=1, keepdims=True)

    def block_rows(b):
        return slice(b * BLOCK, (b + 1) * BLOCK)

    def reduce_start(which, source, target):
        for d, other in [(d, other) for d in farthest_first for other in (0, 1)] + [(0, 1)]:
            slot = (chips - d) % chips * 2 + other - 1
            pltpu.make_async_remote_copy(
                src_ref=source,
                dst_ref=target.at[slot],
                send_sem=far_send.at[which],
                recv_sem=far_recv.at[which],
                device_id=peer(d, other),
                device_id_type=MESH,
            ).start()

    def reduce_finish(which, mine, target):
        pltpu.make_async_copy(target, target, far_recv.at[which]).wait()
        terms = [mine] + [target[i].astype(F32) for i in range(chan_count - 1)]
        while len(terms) > 1:
            terms = [sum(terms[i + 1 : i + 2], terms[i]) for i in range(0, len(terms), 2)]
        return lax.rsqrt(terms[0] * (1.0 / width) + epsilon)

    loads[0].wait()
    for b in range(blocks):
        wide = stream[block_rows(b), :].astype(F32)
        norm[0, b : b + 1, :] = to_row(wide * wide)

    pl.semaphore_wait(barrier, chan_count + seq_count - 2)
    own[0] = norm[0].astype(BF16)
    reduce_start(0, own.at[0], gather.at[0])

    def to_next(source, target, i):
        return pltpu.make_async_remote_copy(
            src_ref=source,
            dst_ref=target,
            send_sem=halo_send.at[i],
            recv_sem=halo_recv.at[i],
            device_id={"seq": lax.rem(place + 1, seq_count)},
            device_id_type=MESH,
        )

    last = pl.ds(rows - BLOCK, BLOCK)
    halos = [
        to_next(stream_h.at[last], halo_stream, 0),
        to_next(kmr_h.at[last], halo_kmr, 1),
        to_next(edge, halo_edge, 2),
    ]

    @pl.when(place < seq_count - 1)
    def _():
        halos[0].start()
        halos[1].start()

    loads[1].wait()
    loads[2].wait()
    rates = lam[...]
    weights = res[...] * jnp.sqrt(one_minus_exp(2.0 * rates))
    step_decay = jnp.exp(-float(BLOCK) * rates)
    leap = jnp.exp(-float(rows - BLOCK) * rates)
    offsets = lax.broadcasted_iota(jnp.int32, (BLOCK, chans), 0).astype(F32)
    for m in range(modes):
        step_b[m] = jnp.broadcast_to(step_decay[m : m + 1], (8, chans))
        weight_b[m] = jnp.broadcast_to(weights[m : m + 1], (8, chans))
        leap_b[m] = jnp.broadcast_to(leap[m : m + 1], (8, chans))

    @pl.loop(0, modes)
    def _(m):
        rate = lam[pl.ds(m, 1), :]
        fall[m] = jnp.exp(-rate * offsets) * weight_b[m, 0:1]
        rise[m] = jnp.exp(-rate * (float(BLOCK - 1) - offsets))

    segment[0:BLOCK] = jnp.zeros((BLOCK, chans), F32)
    for tile in range(chans // LANES):
        lanes = slice(tile * LANES, (tile + 1) * LANES)

        @pl.loop(0, BLOCK // 8)
        def _(r):
            spot = pl.multiple_of(r * 8, 8)
            terms = [fall[m, pl.ds(spot, 8), lanes] for m in range(modes)]
            for b in range(blocks):
                total = terms[0]
                for m in range(1, modes):
                    total = total + terms[m]
                segment[pl.ds(pl.multiple_of((b + 1) * BLOCK + spot, 8), 8), lanes] = total
                if b < blocks - 1:
                    terms = [terms[m] * step_b[m, :, lanes] for m in range(modes)]

    for load in loads[3:6]:
        load.wait()
    spec_mr[...] = matmul(fwd[:, :BLOCK], taps[...]) + matmul(fwd[:, POINTS : POINTS + BLOCK], taps[...])

    @pl.loop(0, blocks)
    def _(d):
        window = segment[pl.ds(pl.multiple_of(d * BLOCK, BLOCK), POINTS), :]
        spec_h[d] = matmul(fwd[...], pieces(window))

    for load in loads[6:9]:
        load.wait()
    for b in range(blocks):
        here = block_rows(b)
        value[b] = kmr[here, :].astype(F32) * (stream[here, :].astype(F32) * gmr[...])

    @pl.when(place > 0)
    def _():
        halos[0].wait_recv()
        halos[1].wait_recv()
        raw_halo[...] = halo_kmr[...].astype(F32) * (halo_stream[...].astype(F32) * gmr[...])

    norm[0] = reduce_finish(0, norm[0], gather.at[0])
    edge[...] = norm[0, blocks - 1 :, :]

    @pl.when(place < seq_count - 1)
    def _():
        halos[2].start()

    def gate_block(b):
        gated[block_rows(b + 1), :] = (value[b] * to_column(norm[0, b : b + 1, :])).astype(BF16)

    def mr_forward(b):
        spec[b] = matmul(fwd[:, :POINTS], gated[b * BLOCK : b * BLOCK + POINTS, :])

    def mr_inverse(b):
        for r in range(0, BLOCK, 16):
            upper, lower = slice(r, r + 16), slice(BLOCK + r, BLOCK + r + 16)
            re, im = spec[b, upper, :], spec[b, lower, :]
            tap_re, tap_im = spec_mr[upper, :], spec_mr[lower, :]
            product[b, upper, :] = (re * tap_re - im * tap_im).astype(BF16)
            product[b, lower, :] = (re * tap_im + im * tap_re).astype(BF16)
        base[b] = matmul(inv[...], product[b])

    def mr_output(b):
        here = block_rows(b)
        out = (qmr[here, :].astype(F32) * base[b]).astype(BF16)
        mr[here, :] = out
        mix = (stream[here, :].astype(F32) + out.astype(F32)).astype(BF16)
        mixed[here, :] = mix
        wide = mix.astype(F32)
        norm[1, b : b + 1, :] = to_row(wide * wide)

    for turn in range(blocks + 3):
        if turn < blocks:
            gate_block(turn)
        for lag, step in ((0, mr_forward), (1, mr_inverse), (2, mr_output)):
            if 1 <= turn - lag < blocks:
                step(turn - lag)
    norm[1, 0:1, :] = jnp.zeros((1, BLOCK), F32)
    own[1] = norm[1].astype(BF16)
    reduce_start(1, own.at[1], gather.at[1])

    @pl.when(place == 0)
    def _():
        gated[0:BLOCK] = jnp.zeros((BLOCK, chans), BF16)

    @pl.when(place > 0)
    def _():
        halos[2].wait_recv()
        gated[0:BLOCK] = (raw_halo[...] * to_column(halo_edge[...])).astype(BF16)

    mr_forward(0)
    mr_inverse(0)
    mr_output(0)
    own_first[...] = norm[1, 0:1, :].astype(BF16)
    reduce_start(2, own_first, gather_first)

    for load in loads[9:]:
        load.wait()
    for b in range(blocks):
        here = block_rows(b)
        value[b] = kli[here, :].astype(F32) * (mixed[here, :].astype(F32) * gli[...])

    def widen(row):
        return jnp.broadcast_to(to_column(row), (BLOCK, LANES))

    first = norm[1, 0:1, :]
    norm[1] = reduce_finish(1, norm[1], gather.at[1])
    for b in range(1, blocks):
        scale[b] = widen(norm[1, b : b + 1, :])

    for tile in range(chans // LANES):
        lanes = slice(tile * LANES, (tile + 1) * LANES)

        def collect(r, totals, lanes=lanes):
            spot = pl.ds(pl.multiple_of(r * 8, 8), 8)
            items = [value[b, spot, lanes] * scale[b, spot, :] for b in range(1, blocks)]
            result = []
            for m in range(modes):
                decay = step_b[m, :, lanes]
                total = items[0]
                for item in items[1:]:
                    total = total * decay + item
                result.append(totals[m] + total * rise[m, spot, lanes])
            return tuple(result)

        totals = lax.fori_loop(
            0, BLOCK // 8, collect, tuple(jnp.zeros((8, LANES), F32) for _ in range(modes))
        )
        for m in range(modes):
            held[m, :, lanes] = totals[m]

    scale[0] = widen(reduce_finish(2, first, gather_first))

    def state_copy(target):
        return pltpu.make_async_remote_copy(
            src_ref=state,
            dst_ref=states.at[place],
            send_sem=state_send.at[target],
            recv_sem=state_recv.at[place],
            device_id={"seq": target},
            device_id_type=MESH,
        )

    for tile in range(chans // LANES):
        lanes = slice(tile * LANES, (tile + 1) * LANES)

        def collect_first(r, totals, lanes=lanes):
            spot = pl.ds(pl.multiple_of(r * 8, 8), 8)
            item = value[0, spot, lanes] * scale[0, spot, :]
            return tuple(totals[m] + item * rise[m, spot, lanes] for m in range(modes))

        totals = lax.fori_loop(
            0, BLOCK // 8, collect_first, tuple(jnp.zeros((8, LANES), F32) for _ in range(modes)), unroll=4
        )
        for m in range(modes):
            total = held[m, :, lanes] + totals[m] * leap_b[m, :, lanes]
            state_wide[m : m + 1, :] = jnp.sum(total, axis=0, keepdims=True)
        state[tile] = state_wide[...].astype(BF16)

    @pl.loop(0, seq_count - 1 - place)
    def _(i):
        state_copy(seq_count - 1 - i).start()

    for b in range(blocks):
        value[b] = value[b] * jnp.concatenate([scale[b]] * (chans // LANES), axis=1)
        spec[b] = matmul(fwd[:, :BLOCK], value[b].astype(BF16))

    for tile in range(chans // LANES):
        lanes = slice(tile * LANES, (tile + 1) * LANES)

        @pl.loop(0, BLOCK // 8)
        def _(r):
            upper = pl.ds(pl.multiple_of(r * 8, 8), 8)
            lower = pl.ds(pl.multiple_of(BLOCK + r * 8, 8), 8)
            h_re = [spec_h[d, upper, lanes] for d in range(blocks)]
            h_im = [spec_h[d, lower, lanes] for d in range(blocks)]
            v_re = [spec[b, upper, lanes] for b in range(blocks)]
            v_im = [spec[b, lower, lanes] for b in range(blocks)]
            for b in range(blocks):
                re = h_re[0] * v_re[b] - h_im[0] * v_im[b]
                im = h_re[0] * v_im[b] + h_im[0] * v_re[b]
                for d in range(1, b + 1):
                    re = re + (h_re[d] * v_re[b - d] - h_im[d] * v_im[b - d])
                    im = im + (h_re[d] * v_im[b - d] + h_im[d] * v_re[b - d])
                spec[b, upper, lanes] = re
                spec[b, lower, lanes] = im

    for b in range(blocks):
        base[b] = matmul(inv[...], spec[b].astype(BF16)) + skip[...] * value[b]

    through = jnp.exp(-float(rows) * rates)

    def take(q, totals):
        pltpu.make_async_copy(states.at[q], states.at[q], state_recv.at[q]).wait()
        return tuple(
            total * through[:, tile * LANES : (tile + 1) * LANES] + states[q, tile].astype(F32)
            for tile, total in enumerate(totals)
        )

    tiles = range(chans // LANES)
    incoming = lax.fori_loop(0, place, take, tuple(jnp.zeros((modes, LANES), F32) for _ in tiles))
    for tile in tiles:
        lanes = slice(tile * LANES, (tile + 1) * LANES)
        lead = incoming[tile] * jnp.exp(-rates[:, lanes])
        for m in range(modes):
            lead_b[m, :, lanes] = jnp.broadcast_to(lead[m : m + 1], (8, LANES))

    @pl.when(place < seq_count - 1)
    def _():
        for halo in halos:
            halo.wait_send()

    for which, others in enumerate((gather.at[0], gather.at[1], gather_first)):
        pltpu.make_async_copy(others, others, far_send.at[which]).wait()

    @pl.loop(place + 1, seq_count)
    def _(target):
        state_copy(target).wait_send()


def last_kernel(mr, base, fall, lead_b, step_b, qli, mr_h, li_h, li, store_sem):
    modes, _, chans = fall.shape
    blocks = base.shape[0]
    stores = [pltpu.make_async_copy(mr, mr_h, store_sem.at[0])]
    stores[0].start()
    for tile in range(chans // LANES):
        lanes = slice(tile * LANES, (tile + 1) * LANES)

        @pl.loop(0, BLOCK // 16)
        def _(r):
            outs = [[None, None] for _ in range(blocks)]
            for part_index in range(2):
                spot = pl.ds(pl.multiple_of(r * 16 + part_index * 8, 8), 8)
                totals = [base[b, spot, lanes] for b in range(blocks)]
                for group in (range(modes // 2), range(modes // 2, modes)):
                    terms = [fall[m, spot, lanes] * lead_b[m, :, lanes] for m in group]
                    steps = [step_b[m, :, lanes] for m in group]
                    for b in range(blocks):
                        pairs = terms
                        while len(pairs) > 1:
                            pairs = [sum(pairs[i + 1 : i + 2], pairs[i]) for i in range(0, len(pairs), 2)]
                        totals[b] = totals[b] + pairs[0]
                        if b < blocks - 1:
                            terms = [term * step for term, step in zip(terms, steps)]
                for b in range(blocks):
                    outs[b][part_index] = totals[b]
            for b in range(blocks):
                here = pl.ds(pl.multiple_of(b * BLOCK + r * 16, 16), 16)
                total = jnp.concatenate(outs[b], axis=0)
                li[here, lanes] = (qli[here, lanes].astype(F32) * total).astype(BF16)

        store = pltpu.make_async_copy(li.at[:, lanes], li_h.at[:, lanes], store_sem.at[1 + tile])
        store.start()
        stores.append(store)
    for store in stores:
        store.wait()


def shards(seq_count, chan_count, width, *args):
    (stream, qmr, kmr, taps, gmr, qli, kli, gli, lam, res, skip) = args
    rows, chans = stream.shape
    modes = lam.shape[0]
    blocks = rows // BLOCK
    gmr, gli, skip = (a.reshape(1, chans) for a in (gmr, gli, skip))
    operands = (stream, qmr, kmr, taps, gmr, qli, kli, gli, lam, res, skip) + transform_tables()
    vmem = pltpu.VMEM
    dma = pltpu.SemaphoreType.DMA
    passed = [
        vmem((rows, chans), BF16),
        vmem((blocks, BLOCK, chans), F32),
        vmem((modes, BLOCK, chans), F32),
        vmem((modes, 8, chans), F32),
        vmem((modes, 8, chans), F32),
        vmem((rows, chans), BF16),
    ]
    handed = pl.pallas_call(
        functools.partial(main_kernel, seq_count, chan_count, width),
        out_shape=passed,
        in_specs=[pl.BlockSpec(memory_space=pltpu.HBM)] * len(operands),
        out_specs=[pl.BlockSpec(memory_space=vmem)] * len(passed),
        scratch_shapes=[vmem(a.shape, a.dtype) for a in operands if a is not qli]
        + [
            vmem((rows + BLOCK, chans), BF16),
            vmem((rows, chans), BF16),
            vmem((blocks, BLOCK, chans), F32),
            vmem((modes, BLOCK, chans), F32),
            vmem((rows + BLOCK, chans), F32),
            vmem((blocks, POINTS, chans), F32),
            vmem((POINTS, chans), F32),
            vmem((blocks, POINTS, chans), F32),
            vmem((blocks, POINTS, chans), BF16),
            vmem((modes, 8, chans), F32),
            vmem((modes, 8, chans), F32),
            vmem((BLOCK, chans), F32),
            vmem((blocks, BLOCK, LANES), F32),
            vmem((modes, 8, chans), F32),
            vmem((2, blocks, BLOCK), F32),
            vmem((2, blocks, BLOCK), BF16),
            vmem((2, chan_count - 1, blocks, BLOCK), BF16),
            vmem((1, BLOCK), BF16),
            vmem((chan_count - 1, 1, BLOCK), BF16),
            vmem((BLOCK, chans), BF16),
            vmem((BLOCK, chans), BF16),
            vmem((1, BLOCK), F32),
            vmem((1, BLOCK), F32),
            vmem((modes, LANES), F32),
            vmem((chans // LANES, modes, LANES), BF16),
            vmem((seq_count, chans // LANES, modes, LANES), BF16),
            dma((len(operands),)),
            dma((3,)),
            dma((3,)),
            dma((3,)),
            dma((3,)),
            dma((seq_count,)),
            dma((seq_count,)),
        ],
        compiler_params=pltpu.CompilerParams(
            collective_id=0, has_side_effects=True, vmem_limit_bytes=36 * 2**20
        ),
    )(*(pltpu.with_memory_space_constraint(a, pltpu.HBM) for a in operands))
    return tuple(
        pl.pallas_call(
            last_kernel,
            out_shape=[jax.ShapeDtypeStruct((rows, chans), BF16)] * 2,
            in_specs=[pl.BlockSpec(memory_space=vmem)] * len(passed),
            out_specs=[pl.BlockSpec(memory_space=pltpu.HBM)] * 2,
            scratch_shapes=[vmem((rows, chans), BF16), dma((3,))],
            compiler_params=pltpu.CompilerParams(vmem_limit_bytes=8 * 2**20),
        )(*handed)
    )


def solution(mesh):
    wide, per_channel, table = P("seq", "chan"), P("chan"), P(None, "chan")
    seq_count, chan_count = mesh.shape["seq"], mesh.shape["chan"]

    def whole(*args):
        width = args[0].shape[1]
        return jax.shard_map(
            functools.partial(shards, seq_count, chan_count, width),
            mesh=mesh,
            in_specs=(wide, wide, wide, table, per_channel, wide, wide, per_channel, table, table, per_channel),
            out_specs=(wide, wide),
            check_vma=False,
        )(*args)

    return whole
```

```python
import functools

import jax
import jax.numpy as jnp
import numpy as np
from jax import lax
from jax.experimental import pallas as pl
from jax.experimental.pallas import tpu as pltpu
from jax.sharding import PartitionSpec as P

MESH = pl.DeviceIdType.MESH
F32 = jnp.float32
BF16 = jnp.bfloat16
epsilon = 1e-06

BLOCK = 128
POINTS = 2 * BLOCK
LANES = 128


def transform_tables():
    turns = (2 * np.arange(BLOCK)[:, None] + 1) * np.arange(POINTS)[None, :] % (2 * POINTS)
    angle = turns * (np.pi / POINTS)
    forward = np.concatenate([np.cos(angle), -np.sin(angle)], axis=0)
    inverse = (2.0 / POINTS) * forward[:, BLOCK:].T
    high = forward.astype(BF16)
    low = (forward - high.astype(np.float64)).astype(BF16)
    return np.concatenate([high, low, high], axis=1), inverse.astype(BF16)


def pieces(value):
    high = value.astype(BF16)
    low = (value - high.astype(F32)).astype(BF16)
    return jnp.concatenate([high, high, low], axis=0)


def matmul(a, b):
    return jnp.dot(a, b, preferred_element_type=F32)


def one_minus_exp(x):
    series = jnp.ones_like(x)
    for n in range(11, 1, -1):
        series = 1.0 - x * (1.0 / n) * series
    return jnp.where(x < 0.5, x * series, 1.0 - jnp.exp(-x))


def main_kernel(
    seq_count, chan_count, width,
    stream_h, qmr_h, kmr_h, taps_h, gmr_h, qli_h, kli_h, gli_h, lam_h, res_h, skip_h, fwd_h, inv_h,
    mr, base, fall, lead_b, step_b, qli,
    stream, qmr, kmr, taps, gmr, kli, gli, lam, res, skip, fwd, inv,
    gated, mixed, value, rise, segment, spec_h, spec_mr, spec, product, weight_b, leap_b, raw_halo, scale, held,
    norm, own, gather, own_first, gather_first, halo_stream, halo_kmr, edge, halo_edge, state_wide, state, states,
    load_sem, far_send, far_recv, halo_send, halo_recv, state_send, state_recv,
):
    rows, chans = stream.shape
    blocks = rows // BLOCK
    modes = lam.shape[0]
    place = lax.axis_index("seq")
    chan = lax.axis_index("chan")
    core = lax.rem(chan, 2)
    chips = chan_count // 2

    loads = [
        pltpu.make_async_copy(source, target, load_sem.at[i])
        for i, (source, target) in enumerate(
            [
                (stream_h, stream), (lam_h, lam), (res_h, res), (taps_h, taps), (fwd_h, fwd), (inv_h, inv),
                (kmr_h, kmr), (gmr_h, gmr), (qmr_h, qmr), (kli_h, kli), (gli_h, gli), (skip_h, skip), (qli_h, qli),
            ]
        )
    ]
    loads[0].start()

    barrier = pltpu.get_barrier_semaphore()

    farthest_first = sorted(range(1, chips), key=lambda d: -min(d, chips - d))

    def peer(chip_step, other):
        return {"chan": lax.rem(chan + 2 * chip_step, chan_count) + other * (1 - 2 * core)}

    for d, other in [(d, other) for d in farthest_first for other in (0, 1)] + [(0, 1)]:
        pl.semaphore_signal(barrier, inc=1, device_id=peer(d, other), device_id_type=MESH)

    @pl.loop(1, seq_count)
    def _(i):
        pl.semaphore_signal(
            barrier, inc=1, device_id={"seq": lax.rem(place + i, seq_count)}, device_id_type=MESH
        )

    for load in loads[1:]:
        load.start()

    diagonal = (
        lax.broadcasted_iota(jnp.int32, (BLOCK, BLOCK), 0) == lax.broadcasted_iota(jnp.int32, (BLOCK, BLOCK), 1)
    )

    def to_row(wide):
        total = jnp.sum(wide, axis=1, keepdims=True)
        return jnp.sum(jnp.where(diagonal, total, 0.0), axis=0, keepdims=True)

    def to_column(row):
        return jnp.sum(jnp.where(diagonal, row, 0.0), axis=1, keepdims=True)

    def block_rows(b):
        return slice(b * BLOCK, (b + 1) * BLOCK)

    def reduce_start(which, source, target):
        for d, other in [(d, other) for d in farthest_first for other in (0, 1)] + [(0, 1)]:
            slot = (chips - d) % chips * 2 + other - 1
            pltpu.make_async_remote_copy(
                src_ref=source,
                dst_ref=target.at[slot],
                send_sem=far_send.at[which],
                recv_sem=far_recv.at[which],
                device_id=peer(d, other),
                device_id_type=MESH,
            ).start()

    def reduce_finish(which, mine, target):
        pltpu.make_async_copy(target, target, far_recv.at[which]).wait()
        terms = [mine] + [target[i].astype(F32) for i in range(chan_count - 1)]
        while len(terms) > 1:
            terms = [sum(terms[i + 1 : i + 2], terms[i]) for i in range(0, len(terms), 2)]
        return lax.rsqrt(terms[0] * (1.0 / width) + epsilon)

    loads[0].wait()
    for b in range(blocks):
        wide = stream[block_rows(b), :].astype(F32)
        norm[0, b : b + 1, :] = to_row(wide * wide)

    pl.semaphore_wait(barrier, chan_count + seq_count - 2)
    own[0] = norm[0].astype(BF16)
    reduce_start(0, own.at[0], gather.at[0])

    def to_next(source, target, i):
        return pltpu.make_async_remote_copy(
            src_ref=source,
            dst_ref=target,
            send_sem=halo_send.at[i],
            recv_sem=halo_recv.at[i],
            device_id={"seq": lax.rem(place + 1, seq_count)},
            device_id_type=MESH,
        )

    last = pl.ds(rows - BLOCK, BLOCK)
    halos = [
        to_next(stream_h.at[last], halo_stream, 0),
        to_next(kmr_h.at[last], halo_kmr, 1),
        to_next(edge, halo_edge, 2),
    ]

    @pl.when(place < seq_count - 1)
    def _():
        halos[0].start()
        halos[1].start()

    loads[1].wait()
    loads[2].wait()
    rates = lam[...]
    weights = res[...] * jnp.sqrt(one_minus_exp(2.0 * rates))
    step_decay = jnp.exp(-float(BLOCK) * rates)
    leap = jnp.exp(-float(rows - BLOCK) * rates)
    offsets = lax.broadcasted_iota(jnp.int32, (BLOCK, chans), 0).astype(F32)
    for m in range(modes):
        step_b[m] = jnp.broadcast_to(step_decay[m : m + 1], (8, chans))
        weight_b[m] = jnp.broadcast_to(weights[m : m + 1], (8, chans))
        leap_b[m] = jnp.broadcast_to(leap[m : m + 1], (8, chans))

    @pl.loop(0, modes)
    def _(m):
        rate = lam[pl.ds(m, 1), :]
        fall[m] = jnp.exp(-rate * offsets) * weight_b[m, 0:1]
        rise[m] = jnp.exp(-rate * (float(BLOCK - 1) - offsets))

    segment[0:BLOCK] = jnp.zeros((BLOCK, chans), F32)
    for tile in range(chans // LANES):
        lanes = slice(tile * LANES, (tile + 1) * LANES)

        @pl.loop(0, BLOCK // 8)
        def _(r):
            spot = pl.multiple_of(r * 8, 8)
            terms = [fall[m, pl.ds(spot, 8), lanes] for m in range(modes)]
            for b in range(blocks):
                total = terms[0]
                for m in range(1, modes):
                    total = total + terms[m]
                segment[pl.ds(pl.multiple_of((b + 1) * BLOCK + spot, 8), 8), lanes] = total
                if b < blocks - 1:
                    terms = [terms[m] * step_b[m, :, lanes] for m in range(modes)]

    for load in loads[3:6]:
        load.wait()
    spec_mr[...] = matmul(fwd[:, :BLOCK], taps[...]) + matmul(fwd[:, POINTS : POINTS + BLOCK], taps[...])

    @pl.loop(0, blocks)
    def _(d):
        window = segment[pl.ds(pl.multiple_of(d * BLOCK, BLOCK), POINTS), :]
        spec_h[d] = matmul(fwd[...], pieces(window))

    for load in loads[6:9]:
        load.wait()
    for b in range(blocks):
        here = block_rows(b)
        value[b] = kmr[here, :].astype(F32) * (stream[here, :].astype(F32) * gmr[...])

    @pl.when(place > 0)
    def _():
        halos[0].wait_recv()
        halos[1].wait_recv()
        raw_halo[...] = halo_kmr[...].astype(F32) * (halo_stream[...].astype(F32) * gmr[...])

    norm[0] = reduce_finish(0, norm[0], gather.at[0])
    edge[...] = norm[0, blocks - 1 :, :]

    @pl.when(place < seq_count - 1)
    def _():
        halos[2].start()

    def gate_block(b):
        gated[block_rows(b + 1), :] = (value[b] * to_column(norm[0, b : b + 1, :])).astype(BF16)

    def mr_forward(b):
        spec[b] = matmul(fwd[:, :POINTS], gated[b * BLOCK : b * BLOCK + POINTS, :])

    def mr_inverse(b):
        for r in range(0, BLOCK, 16):
            upper, lower = slice(r, r + 16), slice(BLOCK + r, BLOCK + r + 16)
            re, im = spec[b, upper, :], spec[b, lower, :]
            tap_re, tap_im = spec_mr[upper, :], spec_mr[lower, :]
            product[b, upper, :] = (re * tap_re - im * tap_im).astype(BF16)
            product[b, lower, :] = (re * tap_im + im * tap_re).astype(BF16)
        base[b] = matmul(inv[...], product[b])

    def mr_output(b):
        here = block_rows(b)
        out = (qmr[here, :].astype(F32) * base[b]).astype(BF16)
        mr[here, :] = out
        mix = (stream[here, :].astype(F32) + out.astype(F32)).astype(BF16)
        mixed[here, :] = mix
        wide = mix.astype(F32)
        norm[1, b : b + 1, :] = to_row(wide * wide)

    gate_block(0)
    for step in (gate_block, mr_forward, mr_inverse, mr_output):
        for b in range(1, blocks):
            step(b)
    norm[1, 0:1, :] = jnp.zeros((1, BLOCK), F32)
    own[1] = norm[1].astype(BF16)
    reduce_start(1, own.at[1], gather.at[1])

    @pl.when(place == 0)
    def _():
        gated[0:BLOCK] = jnp.zeros((BLOCK, chans), BF16)

    @pl.when(place > 0)
    def _():
        halos[2].wait_recv()
        gated[0:BLOCK] = (raw_halo[...] * to_column(halo_edge[...])).astype(BF16)

    mr_forward(0)
    mr_inverse(0)
    mr_output(0)
    own_first[...] = norm[1, 0:1, :].astype(BF16)
    reduce_start(2, own_first, gather_first)

    for load in loads[9:]:
        load.wait()
    for b in range(blocks):
        here = block_rows(b)
        value[b] = kli[here, :].astype(F32) * (mixed[here, :].astype(F32) * gli[...])

    def widen(row):
        return jnp.broadcast_to(to_column(row), (BLOCK, LANES))

    first = norm[1, 0:1, :]
    norm[1] = reduce_finish(1, norm[1], gather.at[1])
    for b in range(1, blocks):
        scale[b] = widen(norm[1, b : b + 1, :])

    for tile in range(chans // LANES):
        lanes = slice(tile * LANES, (tile + 1) * LANES)

        def collect(r, totals, lanes=lanes):
            spot = pl.ds(pl.multiple_of(r * 8, 8), 8)
            items = [value[b, spot, lanes] * scale[b, spot, :] for b in range(1, blocks)]
            result = []
            for m in range(modes):
                decay = step_b[m, :, lanes]
                total = items[0]
                for item in items[1:]:
                    total = total * decay + item
                result.append(totals[m] + total * rise[m, spot, lanes])
            return tuple(result)

        totals = lax.fori_loop(
            0, BLOCK // 8, collect, tuple(jnp.zeros((8, LANES), F32) for _ in range(modes))
        )
        for m in range(modes):
            held[m, :, lanes] = totals[m]

    scale[0] = widen(reduce_finish(2, first, gather_first))

    def state_copy(target):
        return pltpu.make_async_remote_copy(
            src_ref=state,
            dst_ref=states.at[place],
            send_sem=state_send.at[target],
            recv_sem=state_recv.at[place],
            device_id={"seq": target},
            device_id_type=MESH,
        )

    for tile in range(chans // LANES):
        lanes = slice(tile * LANES, (tile + 1) * LANES)

        def collect_first(r, totals, lanes=lanes):
            spot = pl.ds(pl.multiple_of(r * 8, 8), 8)
            item = value[0, spot, lanes] * scale[0, spot, :]
            return tuple(totals[m] + item * rise[m, spot, lanes] for m in range(modes))

        totals = lax.fori_loop(
            0, BLOCK // 8, collect_first, tuple(jnp.zeros((8, LANES), F32) for _ in range(modes)), unroll=4
        )
        for m in range(modes):
            total = held[m, :, lanes] + totals[m] * leap_b[m, :, lanes]
            state_wide[m : m + 1, :] = jnp.sum(total, axis=0, keepdims=True)
        state[tile] = state_wide[...].astype(BF16)

    @pl.loop(0, seq_count - 1 - place)
    def _(i):
        state_copy(seq_count - 1 - i).start()

    for b in range(blocks):
        value[b] = value[b] * jnp.concatenate([scale[b]] * (chans // LANES), axis=1)
        spec[b] = matmul(fwd[:, :BLOCK], value[b].astype(BF16))

    for tile in range(chans // LANES):
        lanes = slice(tile * LANES, (tile + 1) * LANES)

        @pl.loop(0, BLOCK // 8)
        def _(r):
            upper = pl.ds(pl.multiple_of(r * 8, 8), 8)
            lower = pl.ds(pl.multiple_of(BLOCK + r * 8, 8), 8)
            h_re = [spec_h[d, upper, lanes] for d in range(blocks)]
            h_im = [spec_h[d, lower, lanes] for d in range(blocks)]
            v_re = [spec[b, upper, lanes] for b in range(blocks)]
            v_im = [spec[b, lower, lanes] for b in range(blocks)]
            for b in range(blocks):
                re = h_re[0] * v_re[b] - h_im[0] * v_im[b]
                im = h_re[0] * v_im[b] + h_im[0] * v_re[b]
                for d in range(1, b + 1):
                    re = re + (h_re[d] * v_re[b - d] - h_im[d] * v_im[b - d])
                    im = im + (h_re[d] * v_im[b - d] + h_im[d] * v_re[b - d])
                spec[b, upper, lanes] = re
                spec[b, lower, lanes] = im

    for b in range(blocks):
        base[b] = matmul(inv[...], spec[b].astype(BF16)) + skip[...] * value[b]

    through = jnp.exp(-float(rows) * rates)

    def take(q, totals):
        pltpu.make_async_copy(states.at[q], states.at[q], state_recv.at[q]).wait()
        return tuple(
            total * through[:, tile * LANES : (tile + 1) * LANES] + states[q, tile].astype(F32)
            for tile, total in enumerate(totals)
        )

    tiles = range(chans // LANES)
    incoming = lax.fori_loop(0, place, take, tuple(jnp.zeros((modes, LANES), F32) for _ in tiles))
    for tile in tiles:
        lanes = slice(tile * LANES, (tile + 1) * LANES)
        lead = incoming[tile] * jnp.exp(-rates[:, lanes])
        for m in range(modes):
            lead_b[m, :, lanes] = jnp.broadcast_to(lead[m : m + 1], (8, LANES))

    @pl.when(place < seq_count - 1)
    def _():
        for halo in halos:
            halo.wait_send()

    for which, others in enumerate((gather.at[0], gather.at[1], gather_first)):
        pltpu.make_async_copy(others, others, far_send.at[which]).wait()

    @pl.loop(place + 1, seq_count)
    def _(target):
        state_copy(target).wait_send()


def last_kernel(mr, base, fall, lead_b, step_b, qli, mr_h, li_h, li, store_sem):
    modes, _, chans = fall.shape
    blocks = base.shape[0]
    stores = [pltpu.make_async_copy(mr, mr_h, store_sem.at[0])]
    stores[0].start()
    for tile in range(chans // LANES):
        lanes = slice(tile * LANES, (tile + 1) * LANES)

        @pl.loop(0, BLOCK // 16)
        def _(r):
            outs = [[None, None] for _ in range(blocks)]
            for part_index in range(2):
                spot = pl.ds(pl.multiple_of(r * 16 + part_index * 8, 8), 8)
                totals = [base[b, spot, lanes] for b in range(blocks)]
                for group in (range(modes // 2), range(modes // 2, modes)):
                    terms = [fall[m, spot, lanes] * lead_b[m, :, lanes] for m in group]
                    steps = [step_b[m, :, lanes] for m in group]
                    for b in range(blocks):
                        pairs = terms
                        while len(pairs) > 1:
                            pairs = [sum(pairs[i + 1 : i + 2], pairs[i]) for i in range(0, len(pairs), 2)]
                        totals[b] = totals[b] + pairs[0]
                        if b < blocks - 1:
                            terms = [term * step for term, step in zip(terms, steps)]
                for b in range(blocks):
                    outs[b][part_index] = totals[b]
            for b in range(blocks):
                here = pl.ds(pl.multiple_of(b * BLOCK + r * 16, 16), 16)
                total = jnp.concatenate(outs[b], axis=0)
                li[here, lanes] = (qli[here, lanes].astype(F32) * total).astype(BF16)

        store = pltpu.make_async_copy(li.at[:, lanes], li_h.at[:, lanes], store_sem.at[1 + tile])
        store.start()
        stores.append(store)
    for store in stores:
        store.wait()


def shards(seq_count, chan_count, width, *args):
    (stream, qmr, kmr, taps, gmr, qli, kli, gli, lam, res, skip) = args
    rows, chans = stream.shape
    modes = lam.shape[0]
    blocks = rows // BLOCK
    gmr, gli, skip = (a.reshape(1, chans) for a in (gmr, gli, skip))
    operands = (stream, qmr, kmr, taps, gmr, qli, kli, gli, lam, res, skip) + transform_tables()
    vmem = pltpu.VMEM
    dma = pltpu.SemaphoreType.DMA
    passed = [
        vmem((rows, chans), BF16),
        vmem((blocks, BLOCK, chans), F32),
        vmem((modes, BLOCK, chans), F32),
        vmem((modes, 8, chans), F32),
        vmem((modes, 8, chans), F32),
        vmem((rows, chans), BF16),
    ]
    handed = pl.pallas_call(
        functools.partial(main_kernel, seq_count, chan_count, width),
        out_shape=passed,
        in_specs=[pl.BlockSpec(memory_space=pltpu.HBM)] * len(operands),
        out_specs=[pl.BlockSpec(memory_space=vmem)] * len(passed),
        scratch_shapes=[vmem(a.shape, a.dtype) for a in operands if a is not qli]
        + [
            vmem((rows + BLOCK, chans), BF16),
            vmem((rows, chans), BF16),
            vmem((blocks, BLOCK, chans), F32),
            vmem((modes, BLOCK, chans), F32),
            vmem((rows + BLOCK, chans), F32),
            vmem((blocks, POINTS, chans), F32),
            vmem((POINTS, chans), F32),
            vmem((blocks, POINTS, chans), F32),
            vmem((blocks, POINTS, chans), BF16),
            vmem((modes, 8, chans), F32),
            vmem((modes, 8, chans), F32),
            vmem((BLOCK, chans), F32),
            vmem((blocks, BLOCK, LANES), F32),
            vmem((modes, 8, chans), F32),
            vmem((2, blocks, BLOCK), F32),
            vmem((2, blocks, BLOCK), BF16),
            vmem((2, chan_count - 1, blocks, BLOCK), BF16),
            vmem((1, BLOCK), BF16),
            vmem((chan_count - 1, 1, BLOCK), BF16),
            vmem((BLOCK, chans), BF16),
            vmem((BLOCK, chans), BF16),
            vmem((1, BLOCK), F32),
            vmem((1, BLOCK), F32),
            vmem((modes, LANES), F32),
            vmem((chans // LANES, modes, LANES), BF16),
            vmem((seq_count, chans // LANES, modes, LANES), BF16),
            dma((len(operands),)),
            dma((3,)),
            dma((3,)),
            dma((3,)),
            dma((3,)),
            dma((seq_count,)),
            dma((seq_count,)),
        ],
        compiler_params=pltpu.CompilerParams(
            collective_id=0, has_side_effects=True, vmem_limit_bytes=36 * 2**20
        ),
    )(*(pltpu.with_memory_space_constraint(a, pltpu.HBM) for a in operands))
    return tuple(
        pl.pallas_call(
            last_kernel,
            out_shape=[jax.ShapeDtypeStruct((rows, chans), BF16)] * 2,
            in_specs=[pl.BlockSpec(memory_space=vmem)] * len(passed),
            out_specs=[pl.BlockSpec(memory_space=pltpu.HBM)] * 2,
            scratch_shapes=[vmem((rows, chans), BF16), dma((3,))],
            compiler_params=pltpu.CompilerParams(vmem_limit_bytes=8 * 2**20),
        )(*handed)
    )


def solution(mesh):
    wide, per_channel, table = P("seq", "chan"), P("chan"), P(None, "chan")
    seq_count, chan_count = mesh.shape["seq"], mesh.shape["chan"]

    def whole(*args):
        width = args[0].shape[1]
        return jax.shard_map(
            functools.partial(shards, seq_count, chan_count, width),
            mesh=mesh,
            in_specs=(wide, wide, wide, table, per_channel, wide, wide, per_channel, table, table, per_channel),
            out_specs=(wide, wide),
            check_vma=False,
        )(*args)

    return whole
```
